32 devices in a mesh: animal: 8 (over z, y), snp: 4 (over x, core).
Axes of the slice: x: 2, y: 2, z: 4, core: 2. Of those that a mesh axis runs over, the one named last changes fastest.
Arguments:
- genotype: bfloat16 [8192, 32768], P('animal', 'snp')
- allele_freq: float32 [32768], P('snp')
- right_side: float32 [8192, 128], P('animal'), may hold values from -6 to 6
- diagonal: float32 [8192, 128], P('animal'), may hold values from 0.5 to 2
- mendelian: float32 [8192], P('animal'), may hold values from 2 to 4
- genomic_weight: float32 [128], replicated, may hold values from 1 to 8
- send_rows: int32 [8, 8, 64], P('animal'), may hold values from 0 to 1023, as said below
- sire_slot: int32 [8192], P('animal'), may hold values from 0 to 463, as said below
- dam_slot: int32 [8192], P('animal'), may hold values from 16 to 511, as said below
Outputs:
- solution: float32 [8192, 128], P('animal')
- residual: float32 [8192, 128], P('animal')
The draws below stay inside these ranges and needn't reach their ends.
Inputs may be any that keep to these rules, and one draw needn't show every extreme that they name: send_rows[o, d, :] lists 64 distinct local rows of owner o's 1024 animals, those sent to device d. sire_slot[i] = o * 64 + k with k < 16. dam_slot[i] = o * 64 + k with k >= 16.
All inputs are finite; a program needn't handle non-finite values.
Results may differ from the reference program's by a relative error of at most 0.0067.
Values may be sent and summed in bfloat16 or wider, within the bound.
No kernel may reach another device: no remote copies, remote signals or barrier semaphores. Data moves between devices by JAX's collectives and lax.ppermute only.
A program may use at most 64 MiB of HBM per device.

```python
import math
import jax
import jax.numpy as jnp
from jax import lax

ROWS_DEV = 1024
SNPS = 32768
SLOTS = 64
ITERS = 2
COLS = 128
OWNERS = 8
ANIMALS = 8192


def column_percent(key):
    return jax.random.randint(jax.random.fold_in(key, 11), (SNPS,), 5, 51)


def draw_allele_freq(key, part):
    return column_percent(key).astype(jnp.float32) / 100.0


def draw_genotype(key, part):
    percent = column_percent(key)
    joined = jax.random.randint(jax.random.fold_in(key, 12), (ANIMALS, SNPS), 0, 10000)
    first = joined % 100 < percent[None, :]
    second = joined // 100 < percent[None, :]
    codes = first.astype(jnp.int32) + second.astype(jnp.int32)
    return codes.astype(jnp.float32).astype(jnp.bfloat16)


def pedigree_plan(key):
    base = jax.random.fold_in(key, 21)
    scores = jax.random.randint(jax.random.fold_in(base, 1), (OWNERS, OWNERS, ROWS_DEV), 0, 65536)
    scores = scores * ROWS_DEV + jnp.arange(ROWS_DEV, dtype=jnp.int32)[None, None, :]
    order = jnp.argsort(scores, axis=-1)
    send = order[:, :, :SLOTS].astype(jnp.int32)
    first_src = jax.random.randint(jax.random.fold_in(base, 2), (ANIMALS,), 0, OWNERS)
    second_src = jax.random.randint(jax.random.fold_in(base, 3), (ANIMALS,), 0, OWNERS)
    sire_src = jnp.minimum(first_src, second_src)
    sire_within = jax.random.randint(jax.random.fold_in(base, 4), (ANIMALS,), 0, SLOTS // 4)
    dam_src = jax.random.randint(jax.random.fold_in(base, 5), (ANIMALS,), 0, OWNERS)
    dam_within = jax.random.randint(jax.random.fold_in(base, 6), (ANIMALS,), SLOTS // 4, SLOTS)
    sire = (sire_src * SLOTS + sire_within).astype(jnp.int32)
    dam = (dam_src * SLOTS + dam_within).astype(jnp.int32)
    return (send, sire, dam)


def draw_send_rows(key, part):
    return pedigree_plan(key)[0]


def draw_sire_slot(key, part):
    return pedigree_plan(key)[1]


def draw_dam_slot(key, part):
    return pedigree_plan(key)[2]


def block_scale(stream_key, dims, split, low, top_value):
    gain, own = 1.0, jax.random.fold_in(stream_key, 6)
    for position, blocks in split:
        heights = jnp.exp(jax.random.uniform(jax.random.fold_in(own, position), (blocks,), jnp.float32, low / len(split), top_value / len(split)))
        gain = gain * jnp.repeat(heights, dims[position] // blocks).reshape([-1 if axis == position else 1 for axis in range(len(dims))])
    return gain


def bell_draw(rng, extent, spread, bound, shards=(), kind=jnp.bfloat16):
    loudness = block_scale(rng, extent, shards, -0.22, 0.18) if shards else 1.0
    result = jax.random.normal(rng, extent, jnp.float32) * spread * loudness
    return jnp.minimum(jnp.maximum(result, -bound), bound).astype(kind)


def setup_inputs(seed: int = 0) -> dict:
    keys = jax.random.split(jax.random.key(seed), 10)
    genotype = draw_genotype(jax.random.fold_in(keys[9], 71), 0)
    allele_freq = draw_allele_freq(jax.random.fold_in(keys[9], 71), 0)
    right_side = bell_draw(keys[2], (ANIMALS, COLS), 1.0, 6.0, ((0, 8),), jnp.float32)
    diagonal = jnp.clip(jnp.exp(math.log(2.0) - 1.3862944 * jax.random.uniform(keys[3], (ANIMALS, COLS), jnp.float32) ** block_scale(keys[3], (ANIMALS, COLS), ((0, 8),), -0.2, 0.2)), 0.5, 2.0)
    mendelian = jnp.clip(2.0 + 2.0 * jax.random.uniform(keys[4], (ANIMALS,), jnp.float32) ** block_scale(keys[4], (ANIMALS,), ((0, 8),), -0.2, 0.2), 2.0, 4.0)
    genomic_weight = jnp.clip(jnp.exp(jax.random.uniform(keys[5], (COLS,), jnp.float32, math.log(1.0), math.log(8.0))), 1.0, 8.0)
    send_rows = draw_send_rows(jax.random.fold_in(keys[9], 71), 0)
    sire_slot = draw_sire_slot(jax.random.fold_in(keys[9], 71), 0)
    dam_slot = draw_dam_slot(jax.random.fold_in(keys[9], 71), 0)
    return dict(genotype=genotype, allele_freq=allele_freq, right_side=right_side, diagonal=diagonal, mendelian=mendelian, genomic_weight=genomic_weight, send_rows=send_rows, sire_slot=sire_slot, dam_slot=dam_slot)


def reference(genotype, allele_freq, right_side, diagonal, mendelian, genomic_weight, send_rows, sire_slot, dam_slot):
    centered = (genotype.astype(jnp.float32) - 2.0 * allele_freq[None, :]).astype(jnp.bfloat16)
    owner = (jnp.arange(ANIMALS) // ROWS_DEV).astype(jnp.int32)

    def parent(slot):
        source = slot // SLOTS
        within = slot % SLOTS
        return (source * ROWS_DEV + send_rows[source, owner, within]).astype(jnp.int32)

    sire = parent(sire_slot)
    dam = parent(dam_slot)
    scale = genomic_weight[None, :] / SNPS

    def operate(field):
        field_b = field.astype(jnp.bfloat16)
        effects = lax.dot_general(centered, field_b, (((0,), (0,)), ((), ())), preferred_element_type=jnp.float32)
        effects = effects.astype(jnp.bfloat16)
        genomic = jnp.dot(centered, effects, preferred_element_type=jnp.float32)
        mendel_term = mendelian[:, None] * (field - 0.5 * (field[sire] + field[dam]))
        pedigree = mendel_term + jnp.zeros_like(field).at[sire].add(-0.5 * mendel_term).at[dam].add(-0.5 * mendel_term)
        return diagonal * field + pedigree + scale * genomic

    solution = jnp.zeros_like(right_side)
    residual = right_side
    w_field = operate(residual)
    z_field = jnp.zeros_like(right_side)
    s_field = jnp.zeros_like(right_side)
    p_field = jnp.zeros_like(right_side)
    gamma_prev = None
    alpha_prev = None
    for step in range(ITERS):
        gamma = jnp.sum(residual * residual, axis=0)
        delta = jnp.sum(w_field * residual, axis=0)
        q_field = operate(w_field)
        if step == 0:
            beta = jnp.zeros_like(gamma)
            alpha = gamma / delta
        else:
            beta = gamma / gamma_prev
            alpha = gamma / (delta - beta * gamma / alpha_prev)
        z_field = q_field + beta * z_field
        s_field = w_field + beta * s_field
        p_field = residual + beta * p_field
        solution = solution + alpha * p_field
        residual = residual - alpha * s_field
        w_field = w_field - alpha * z_field
        gamma_prev = gamma
        alpha_prev = alpha
    return solution, residual
```

```python
import jax
import jax.numpy as jnp
from jax import lax
from jax.experimental import pallas as pl
from jax.experimental.pallas import tpu as pltpu
from jax.sharding import PartitionSpec as P

ITERS = 2
BF16, F32 = jnp.bfloat16, jnp.float32
LANES = 128
VMEM = pl.BlockSpec(memory_space=pltpu.VMEM)
SMEM = pl.BlockSpec(memory_space=pltpu.SMEM)


def call(body, ins, outs, smem=0, limit=24, scratch=(), alias=None, flops=0):
    outs = tuple(jax.ShapeDtypeStruct(*o) for o in outs)
    moved = sum(a.size * a.dtype.itemsize for a in (*ins, *outs))
    return pl.pallas_call(
        body,
        in_specs=[SMEM] * smem + [VMEM] * (len(ins) - smem),
        out_specs=tuple(VMEM for _ in outs),
        out_shape=outs,
        scratch_shapes=scratch,
        input_output_aliases=alias or {},
        cost_estimate=pl.CostEstimate(flops=flops, bytes_accessed=moved, transcendentals=0),
        compiler_params=pltpu.CompilerParams(vmem_limit_bytes=limit << 20),
    )(*ins)


def positions(order):
    if not order:
        return [0]
    rest = positions(order[1:])
    return rest + [j | order[0] for j in rest]


def swap(x, axis, bit):
    size = lax.axis_size(axis)
    return lax.ppermute(x, axis, [(i, i ^ bit) for i in range(size)])


def total(x, axis):
    bit = 1
    while bit < lax.axis_size(axis):
        x = x + swap(x, axis, bit)
        bit *= 2
    return x


def exchange(send, keep, order):
    for step, bit in enumerate(order):
        if step:
            half = keep.shape[0] // 2
            keep, send = keep[:half], keep[half:]
        keep = jnp.concatenate([keep, swap(send, "animal", bit)], axis=1)
    return keep[0]


def halve(send, keep, order):
    for step, bit in enumerate(order):
        if step:
            half = keep.shape[0] // 2
            keep, send = keep[:half], keep[half:]
        got = swap(send, "animal", bit)
        keep = (keep.astype(F32) + got.astype(F32)).astype(BF16)
    return keep


def double(x, order):
    for bit in reversed(order[1:]):
        x = jnp.concatenate([x, swap(x, "animal", bit)], axis=0)
    return x, swap(x, "animal", order[0])


def index_body(slots, tab, send_rows, sire, dam, gather_hot, parent_hot, index):
    blocks = tab.shape[0]
    for r in range(blocks):
        index[:, pl.ds(r * slots, slots)] = send_rows[pl.ds(tab[r], 1), :]
    rows, wide = gather_hot.shape
    spot = lax.broadcasted_iota(jnp.int32, (rows, wide), 0)
    gather_hot[...] = jnp.where(spot == index[...], 1.0, 0.0).astype(BF16)
    spot = lax.broadcasted_iota(jnp.int32, (wide, rows), 0)
    hot = jnp.where(spot == sire[...], 1.0, 0.0) + jnp.where(spot == dam[...], 1.0, 0.0)
    parent_hot[...] = hot.astype(BF16)


def split_dot(hot, values, dims):
    high = values.astype(BF16)
    low = (values - high.astype(F32)).astype(BF16)
    dims = (dims, ((), ()))
    out = lax.dot_general(hot, high, dims, preferred_element_type=F32)
    return out + lax.dot_general(hot, low, dims, preferred_element_type=F32)


def put_blocks(order, slots, values, send, keep):
    half = send.shape[0]
    for at, r in enumerate(positions(order)):
        block = values[r * slots : (r + 1) * slots]
        if at < half:
            keep[at] = block
        else:
            send[at - half] = block


def emit_field(order, slots, field, gather_hot, flipped, sums, send, keep):
    turned = field.T.astype(BF16)
    flipped[...] = turned
    sums[...] = jnp.broadcast_to(
        jnp.sum(turned.astype(F32), axis=1, keepdims=True), sums.shape
    )
    rows = split_dot(gather_hot[...], field, ((0,), (0,)))
    put_blocks(order, slots, rows, send, keep)


def start_body(order, slots, field, gather_hot, flipped, sums, send, keep):
    emit_field(order, slots, field[...], gather_hot, flipped, sums, send, keep)


def effects_body(parts, part, tab, geno, freq, flipped, sums, send, keep):
    half, _, width = send.shape

    def one(t, out, at):
        col = pl.multiple_of((tab[t] * parts + part) * width, LANES)
        here = pl.ds(col, width)
        acc = jnp.dot(flipped[...], geno[:, here], preferred_element_type=F32)
        out[at] = (acc - sums[:, :1] * (2.0 * freq[:, here])).astype(BF16)

    for at in range(half):
        one(half + at, send, at)
    for at in range(half):
        one(at, keep, at)


def offspring_body(order, slots, field, received, parent_hot, mendelian, term, send, keep):
    hot = parent_hot[...]
    parents = split_dot(hot, received[...], ((0,), (0,)))
    rows, cols = field.shape
    weight = jnp.broadcast_to(mendelian[...], (cols, rows)).T
    mendel = weight * (field[...] - 0.5 * parents)
    term[...] = mendel
    back = split_dot(hot, mendel, ((1,), (0,)))
    put_blocks(order, slots, -0.5 * back, send, keep)


def values_body(parts, part, first, last, tab, *refs):
    geno, freq, near, far = refs[:4]
    side = refs[4:]
    if not first:
        before, side = side[0], side[1:]
    if last:
        core, side = side[0], side[1:]
        own, other, acc = side
    else:
        (acc,) = side
    half, _, width = near.shape
    turned = (((1,), (1,)), ((), ()))
    spread = None
    for t in range(2 * half):
        col = pl.multiple_of((tab[t] * parts + part) * width, LANES)
        here = pl.ds(col, width)
        block = near[t] if t < half else far[t - half]
        twice = 2.0 * freq[:, here]
        high = twice.astype(BF16).astype(F32)
        mid = (twice - high).astype(BF16).astype(F32)
        low = twice - high - mid
        rows = jnp.concatenate([high, mid, low, jnp.zeros((5, width), F32)], axis=0)
        off = lax.dot_general(rows.astype(BF16), block, turned, preferred_element_type=F32)
        spread = off if t == 0 else spread + off
        value = lax.dot_general(geno[:, here], block, turned, preferred_element_type=F32)
        if t == 0:
            acc[...] = value if first else before[...] + value
        else:
            acc[...] += value
    shift = jnp.sum(spread, axis=0, keepdims=True)
    if last:
        rows = own.shape[0]
        at = core[0, 0] * rows
        own[...] = acc[pl.ds(pl.multiple_of(at, rows), rows), :] - shift
        other[...] = acc[pl.ds(pl.multiple_of(rows - at, rows), rows), :] - shift
    else:
        acc[...] = acc[...] - shift


def apply_operator(core, field, diagonal, scale, term, returned, gather_hot, own, other, full):
    rows = own.shape[0]
    at = core[0, 0] * rows
    full[pl.ds(pl.multiple_of(at, rows), rows), :] = own[...]
    full[pl.ds(pl.multiple_of(rows - at, rows), rows), :] = other[...]
    back = split_dot(gather_hot[...], returned[...], ((1,), (0,)))
    return diagonal[...] * field[...] + (term[...] + back) + scale[...] * full[...]


def colsum(x):
    return jnp.sum(x, axis=0, keepdims=True)


def pack_rows(rows):
    wide = rows[0].shape[1]
    return jnp.concatenate([*rows, jnp.zeros((8 - len(rows), wide), F32)], axis=0)


def middle_body(order, slots, core, field, diagonal, scale, term, returned, gather_hot, own, other,
                image, flipped, sums, send, keep, dots, full):
    out = apply_operator(core, field, diagonal, scale, term, returned, gather_hot, own, other, full)
    image[...] = out
    emit_field(order, slots, out, gather_hot, flipped, sums, send, keep)
    dots[...] = pack_rows([colsum(field[...] * field[...]), colsum(out * field[...])])


def second_body(core, field, diagonal, scale, term, returned, gather_hot, own, other, right, dots,
                moved, next_dots, full):
    q = apply_operator(core, field, diagonal, scale, term, returned, gather_hot, own, other, full)
    alpha = dots[0:1, :] / dots[1:2, :]
    residual = right[...] - alpha * field[...]
    w = field[...] - alpha * q
    moved[...] = w
    next_dots[...] = pack_rows([colsum(residual * residual), colsum(w * residual)])


def final_body(right, image, moved, dots, next_dots, solution, residual):
    alpha0 = dots[0:1, :] / dots[1:2, :]
    gamma = next_dots[0:1, :]
    beta = gamma / dots[0:1, :]
    alpha = gamma / (next_dots[1:2, :] - beta * gamma / alpha0)
    first = right[...] - alpha0 * image[...]
    s = moved[...] + beta * image[...]
    p = first + beta * right[...]
    solution[...] = alpha0 * right[...] + alpha * p
    residual[...] = first - alpha * s


def local(genotype, allele_freq, right_side, diagonal, mendelian, genomic_weight, send_rows,
          sire_slot, dam_slot):
    owners = lax.axis_size("animal")
    blocks = lax.axis_size("snp")
    me = lax.axis_index("animal")
    core = (lax.axis_index("snp") % 2).astype(jnp.int32).reshape(1, 1)
    slots = send_rows.shape[2]
    rows, snps = genotype.shape
    cols = right_side.shape[1]
    owned = snps // owners
    half = owners // 2
    parts = max(1, min(4, owned // LANES))
    width = owned // parts
    bits = [1 << b for b in range(owners.bit_length() - 1)]
    flip = [bits[1], bits[0], *bits[2:]]
    orders = [bits if part % 2 == 0 else flip for part in range(parts)]
    relative = jnp.arange(owners, dtype=jnp.int32)

    def table(order):
        return jnp.asarray(positions(order), jnp.int32) ^ me

    tabs = {0: table(bits), 1: table(flip)}
    freq = allele_freq.reshape(1, snps)
    scale = (genomic_weight / (snps * blocks)).reshape(1, cols)

    def moved_slot(slot):
        source = slot // slots
        return ((source ^ me) * slots + slot % slots).reshape(1, rows)

    gather_hot, parent_hot = call(
        lambda *r: index_body(slots, *r),
        (relative ^ me, send_rows[0], moved_slot(sire_slot), moved_slot(dam_slot)),
        (((rows, owners * slots), BF16), ((owners * slots, rows), BF16)),
        smem=1,
        scratch=[pltpu.VMEM((1, owners * slots), jnp.int32)],
    )
    field_outs = (
        ((cols, rows), BF16),
        ((cols, LANES), F32),
        ((half, slots, cols), F32),
        ((half, slots, cols), F32),
    )

    def genomic_and_pedigree(field, flipped, sums, send, keep):
        gathered = []
        work = 2 * rows * cols * owned * owners // parts
        begun = []
        for part, order in enumerate(orders):
            begun.append(call(
                lambda *r, part=part: effects_body(parts, part, *r),
                (tabs[part % 2], genotype, freq, flipped, sums),
                (((half, cols, width), BF16),) * 2,
                smem=1,
                flops=work,
            ))
        received = exchange(send, keep, bits)
        term, send, keep = call(
            lambda *r: offspring_body(bits, slots, *r),
            (field, received, parent_hot, mendelian.reshape(1, rows)),
            (((rows, cols), F32), *field_outs[2:]),
        )
        for part, order in enumerate(orders):
            gathered.append(double(halve(*begun[part], order), order))
        returned = exchange(send, keep, bits)
        acc = None
        for part in range(parts):
            first, last = part == 0, part == parts - 1
            ins = [tabs[part % 2], genotype, freq, *gathered[part]]
            if not first:
                ins.append(acc)
            if last:
                ins.append(core)
            body = lambda *r, part=part, first=first, last=last: values_body(
                parts, part, first, last, *r
            )
            if last:
                own, other = call(
                    value_body_smem(body, len(ins)),
                    (ins[0], ins[-1], *ins[1:-1]),
                    (((rows // 2, cols), F32),) * 2,
                    smem=2,
                    scratch=[pltpu.VMEM((rows, cols), F32)],
                    flops=work,
                )
            else:
                (acc,) = call(
                    body,
                    tuple(ins),
                    (((rows, cols), F32),),
                    smem=1,
                    flops=work,
                )
        value = own + swap(other, "snp", 1)
        bit = 2
        while bit < blocks:
            short = value.astype(BF16)
            value = short.astype(F32) + swap(short, "snp", bit).astype(F32)
            bit *= 2
        return term, returned, value, swap(value, "snp", 1)

    flipped, sums, send, keep = call(
        lambda *r: start_body(bits, slots, *r), (right_side, gather_hot), field_outs
    )
    term, returned, own, other = genomic_and_pedigree(right_side, flipped, sums, send, keep)
    full = [pltpu.VMEM((rows, cols), F32)]
    image, flipped, sums, send, keep, dots = call(
        lambda *r: middle_body(bits, slots, *r),
        (core, right_side, diagonal, scale, term, returned, gather_hot, own, other),
        (((rows, cols), F32), *field_outs, ((8, cols), F32)),
        smem=1,
        scratch=full,
    )
    dots = total(dots, "animal")
    term, returned, own, other = genomic_and_pedigree(image, flipped, sums, send, keep)
    moved, next_dots = call(
        second_body,
        (core, image, diagonal, scale, term, returned, gather_hot, own, other, right_side, dots),
        (((rows, cols), F32), ((8, cols), F32)),
        smem=1,
        scratch=full,
    )
    next_dots = total(next_dots, "animal")
    return call(
        final_body,
        (right_side, image, moved, dots, next_dots),
        (((rows, cols), F32),) * 2,
    )


def value_body_smem(body, count):
    def reordered(tab, core, *refs):
        ins = refs[: count - 2]
        return body(tab, *ins, core, *refs[count - 2 :])

    return reordered


def solution(mesh):
    placed = (
        P("animal", "snp"),
        P("snp"),
        P("animal", None),
        P("animal", None),
        P("animal"),
        P(),
        P("animal", None, None),
        P("animal"),
        P("animal"),
    )
    return jax.shard_map(
        local,
        mesh=mesh,
        in_specs=placed,
        out_specs=(P("animal", None), P("animal", None)),
        check_vma=False,
    )
```

```python
import jax
import jax.numpy as jnp
from jax import lax
from jax.experimental import pallas as pl
from jax.experimental.pallas import tpu as pltpu
from jax.sharding import PartitionSpec as P

ITERS = 2
BF16, F32, I32 = jnp.bfloat16, jnp.float32, jnp.int32
LANES = 128
VMEM = pl.BlockSpec(memory_space=pltpu.VMEM)
SMEM = pl.BlockSpec(memory_space=pltpu.SMEM)
HBM = pl.BlockSpec(memory_space=pltpu.HBM)


def call(body, ins, outs, specs=None, limit=24, scratch=(), flops=0):
    specs = specs or [VMEM] * (len(ins) - 1)
    outs = tuple(o if hasattr(o, "memory_space") else jax.ShapeDtypeStruct(*o) for o in outs)
    moved = sum(a.size * a.dtype.itemsize for a in ins)
    return pl.pallas_call(
        body,
        in_specs=[SMEM, *specs],
        out_specs=tuple(VMEM for _ in outs),
        out_shape=outs,
        scratch_shapes=scratch,
        cost_estimate=pl.CostEstimate(flops=flops, bytes_accessed=moved, transcendentals=0),
        compiler_params=pltpu.CompilerParams(vmem_limit_bytes=limit << 20),
    )(*ins)


def positions(order):
    if not order:
        return [0]
    rest = positions(order[1:])
    return rest + [j | order[0] for j in rest]


def swap(x, axis, bit):
    size = lax.axis_size(axis)
    return lax.ppermute(x, axis, [(i, i ^ bit) for i in range(size)])


def total(x, axis):
    bit = 1
    while bit < lax.axis_size(axis):
        x = x + swap(x, axis, bit)
        bit *= 2
    return x


def colsum(x):
    return jnp.sum(x, axis=0, keepdims=True)


def stack_rows(rows):
    wide = rows[0].shape[1]
    return jnp.concatenate([*rows, jnp.zeros((8 - len(rows), wide), F32)], axis=0)


def split(x):
    high = x.astype(BF16)
    return high, (x - high.astype(F32)).astype(BF16)


def hot_dot(hot, x, dims):
    high, low = split(x)
    dims = (dims, ((), ()))
    out = lax.dot_general(hot, high, dims, preferred_element_type=F32)
    return out + lax.dot_general(hot, low, dims, preferred_element_type=F32)


class Plan:
    def __init__(self, genotype, right_side, send_rows):
        self.owners = lax.axis_size("animal")
        self.rows, self.snps = genotype.shape
        self.cols = right_side.shape[1]
        self.slots = send_rows.shape[2]
        self.half = self.owners // 2
        self.owned = self.snps // self.owners
        self.parts = max(1, min(4, self.owned // LANES))
        self.width = self.owned // self.parts
        self.nb = self.width // LANES
        bits = [1 << b for b in range(self.owners.bit_length() - 1)]
        flip = [bits[1], bits[0], *bits[2:]]
        self.orders = [bits if part % 2 == 0 else flip for part in range(self.parts)]
        self.bits = bits

    def tile(self, count):
        return ((count, LANES, LANES), BF16)

    def message_shapes(self):
        half, nb = self.half, self.nb
        shapes = [self.tile(half * nb + half), self.tile(half * nb), self.tile(half)]
        for _ in range(1, self.parts):
            shapes += [self.tile(half * nb), self.tile(half * nb)]
        return shapes


def pack(plan, doubled):
    high, low = split(doubled)
    row = lax.broadcasted_iota(I32, doubled.shape, 0)
    block = jnp.where((row & (2 * plan.slots - 1)) < plan.slots, high.astype(F32), low.astype(F32))
    return block.astype(BF16)


def put_rows(plan, order, doubled, send, offset, keep):
    blocks = pack(plan, doubled)
    for at, r in enumerate(positions(order)):
        block = blocks[r * LANES : (r + 1) * LANES]
        if at < plan.half:
            keep[at] = block
        else:
            send[offset + at - plan.half] = block


def owner_columns(plan, place, r):
    return pl.ds(pl.multiple_of((place[0] ^ r) * plan.owned, LANES), plan.owned)


def put_effects(plan, place, r, geno, freq, turned, sums, messages):
    here = owner_columns(plan, place, r)
    acc = jnp.dot(turned, geno[:, here], preferred_element_type=F32)
    acc = (acc - sums * (2.0 * freq[:, here])).astype(BF16)
    half, nb = plan.half, plan.nb
    for part, order in enumerate(plan.orders):
        send, keep = messages[0:2] if part == 0 else messages[2 * part + 1 : 2 * part + 3]
        at = positions(order).index(r)
        out, at = (keep, at) if at < half else (send, at - half)
        for b in range(nb):
            first = part * plan.width + b * LANES
            out[at * nb + b] = acc[:, first : first + LANES]


def emit_rows(plan, field, gather_hot, messages):
    rows = hot_dot(gather_hot[...], field, ((0,), (0,)))
    put_rows(plan, plan.bits, rows, messages[0], plan.half * plan.nb, messages[2])


def turn(field):
    turned = field.T.astype(BF16)
    return turned, jnp.sum(turned.astype(F32), axis=1, keepdims=True)


def begin_body(plan, place, geno, freq, right, send_rows, sire, dam,
               kept, gather_hot, parent_hot, *rest):
    messages, (index, sem) = rest[:-2], rest[-2:]
    copies = []
    for r in range(plan.owners):
        here = owner_columns(plan, place, r)
        copies.append(pltpu.make_async_copy(geno.at[:, here], kept.at[:, here], sem.at[r]))
        copies[-1].start()
    me, slots = place[0], plan.slots
    shift = slots.bit_length() - 1

    def moved(slot):
        source = slot >> shift
        return ((source ^ me) << shift) + (slot & (slots - 1))

    sires, dams = moved(sire[...]), moved(dam[...])
    animal = lax.broadcasted_iota(I32, (plan.rows, LANES), 0)
    spot = lax.broadcasted_iota(I32, (LANES, plan.rows), 0) & (slots - 1)
    for r in range(plan.owners):
        here = slice(r * LANES, (r + 1) * LANES)
        line = send_rows[pl.ds(me ^ r, 1), :]
        index[:, :slots] = line
        index[:, slots:] = line
        gather_hot[:, here] = jnp.where(animal == index[...], 1.0, 0.0).astype(BF16)
        hot = jnp.where(spot + r * slots == sires, 1.0, 0.0)
        hot = hot + jnp.where(spot + r * slots == dams, 1.0, 0.0)
        parent_hot[here, :] = hot.astype(BF16)
    emit_rows(plan, right[...], gather_hot, messages)
    turned, sums = turn(right[...])
    for r in reversed(range(plan.owners)):
        copies[r].wait()
        put_effects(plan, place, r, kept, freq, turned, sums, messages)


def merge_body(plan, slots_left, sources, place, got, keep_e, keep_p, send, next_e, next_p):
    nb = plan.nb
    half = slots_left // 2
    count = slots_left * nb
    summed = keep_e[...].astype(F32) + got[0:count].astype(F32)
    summed = summed.astype(BF16)
    next_e[...] = summed[: half * nb]
    send[0 : half * nb] = summed[half * nb :]
    for s in range(2 * sources):
        from_, at = (keep_p, s * slots_left) if s < sources else (
            got, count + (s - sources) * slots_left
        )
        next_p[s * half : (s + 1) * half] = from_[at : at + half]
        send[half * nb + s * half : half * nb + (s + 1) * half] = (
            from_[at + half : at + slots_left]
        )


def offspring_body(plan, second, place, got, keep_e, keep_p, field, parent_hot, mendelian, *rest):
    if second:
        plain_before, term_scale, diagonal, right, dots, *rest = rest
    send, keep_back, term, extra = rest
    nb, half = plan.nb, plan.half
    send[0:nb] = (keep_e[...].astype(F32) + got[0:nb].astype(F32)).astype(BF16)
    received = jnp.concatenate([keep_p[...], got[nb:]], axis=0)
    received = received.reshape(plan.owners * LANES, plan.cols)
    hot = parent_hot[...]
    parents = lax.dot_general(hot, received, (((0,), (0,)), ((), ())), preferred_element_type=F32)
    weight = jnp.broadcast_to(mendelian[...], (plan.cols, plan.rows)).T
    plain = field[...] - 0.5 * parents
    mendel = weight * plain
    term[...] = mendel
    back = -0.5 * hot_dot(hot, mendel, ((1,), (0,)))
    put_rows(plan, plan.bits[::-1], back, send, nb, keep_back)
    if second:
        alpha = dots[0:1, :] / dots[1:2, :]
        residual = right[...] - alpha * field[...]
        moved = plain_before[...] - alpha * plain
        whole = colsum(diagonal[...] * field[...] * residual) + colsum(mendel * moved)
        extra[...] = term_scale[0:1, 0:1] * stack_rows(
            [colsum(residual * residual), colsum(field[...] * residual), whole]
        )
    else:
        extra[...] = plain


def spread_body(plan, slots_held, sources, place, sent, got, keep_p, send, next_p):
    nb, half = plan.nb, plan.half
    count = slots_held * nb
    send[0:count] = sent[0:count]
    send[count : 2 * count] = got[0:count]
    left = half // sources
    keep = left // 2
    for s in range(2 * sources):
        from_, at = (keep_p, s * left) if s < sources else (got, count + (s - sources) * left)
        next_p[s * keep : (s + 1) * keep] = from_[at : at + keep]
        first = 2 * count + s * keep
        send[first : first + keep] = from_[at + keep : at + left]


def effect_dots_body(plan, place, rows, dots, *refs):
    before, now, out = refs[: plan.parts], refs[plan.parts : -1], refs[-1]
    alpha = dots[0:1, :] / dots[1:2, :]
    alpha = jnp.broadcast_to(alpha, (LANES, plan.cols)).T
    acc = None
    for old, new in zip(before, now):
        for b in range(plan.nb):
            e = new[b].astype(F32)
            value = e * (old[b].astype(F32) - alpha * e)
            acc = value if acc is None else acc + value
    side = jnp.sum(acc, axis=1, keepdims=True)
    row = jnp.broadcast_to(side, (plan.cols, LANES)).T[0:1, :]
    out[...] = jnp.concatenate([rows[0:3, :], row, rows[4:8, :]], axis=0)


def values_body(plan, group, first, last, place, geno, freq, *refs):
    pairs, refs = refs[: 2 * len(group)], refs[2 * len(group) :]
    if not first:
        before, *refs = refs
    if last:
        own, other, acc = refs
    else:
        (acc,) = refs
    turned = (((1,), (1,)), ((), ()))
    nb, half = plan.nb, plan.half
    spread, begun = None, False
    for index, part in enumerate(group):
        near, far = pairs[2 * index : 2 * index + 2]
        for at, r in enumerate(positions(plan.orders[part])):
            col = pl.multiple_of((place[0] ^ r) * plan.owned + part * plan.width, LANES)
            here = pl.ds(col, plan.width)
            held, at = (near, at) if at < half else (far, at - half)
            block = jnp.concatenate([held[at * nb + b] for b in range(nb)], axis=1)
            twice = 2.0 * freq[:, here]
            high = twice.astype(BF16).astype(F32)
            mid = (twice - high).astype(BF16).astype(F32)
            low = twice - high - mid
            lines = jnp.concatenate([high, mid, low, jnp.zeros((5, plan.width), F32)], axis=0)
            off = lax.dot_general(lines.astype(BF16), block, turned, preferred_element_type=F32)
            spread = off if spread is None else spread + off
            value = lax.dot_general(geno[:, here], block, turned, preferred_element_type=F32)
            if begun:
                acc[...] += value
            else:
                acc[...] = value if first else before[...] + value
                begun = True
    shift = colsum(spread)
    if last:
        rows = own.shape[0]
        at = place[1] * rows
        own[...] = acc[pl.ds(pl.multiple_of(at, rows), rows), :] - shift
        other[...] = acc[pl.ds(pl.multiple_of(rows - at, rows), rows), :] - shift
    else:
        acc[...] = acc[...] - shift


def apply_operator(plan, place, field, diagonal, scale, term, keep_p, got, gather_hot, own, other,
                   full):
    rows = own.shape[0]
    at = place[1] * rows
    full[pl.ds(pl.multiple_of(at, rows), rows), :] = own[...]
    full[pl.ds(pl.multiple_of(rows - at, rows), rows), :] = other[...]
    back = None
    start = plan.half * plan.nb
    for i, r in enumerate(positions(plan.bits)):
        block = keep_p[i] if i < plan.half else got[start + i - plan.half]
        hot = gather_hot[:, r * LANES : (r + 1) * LANES]
        value = jnp.dot(hot, block, preferred_element_type=F32)
        back = value if back is None else back + value
    return diagonal[...] * field[...] + (term[...] + back) + scale[...] * full[...]


def middle_body(plan, place, field, diagonal, scale, term, keep_p, got, gather_hot, own, other,
                geno, freq, image, dots, *rest):
    messages, full = rest[:-1], rest[-1]
    out = apply_operator(
        plan, place, field, diagonal, scale, term, keep_p, got, gather_hot, own, other, full
    )
    image[...] = out
    turned, sums = turn(out)
    for r in reversed(range(plan.owners)):
        put_effects(plan, place, r, geno, freq, turned, sums, messages)
    emit_rows(plan, image[...], gather_hot, messages)
    dots[...] = stack_rows([colsum(field[...] * field[...]), colsum(image[...] * field[...])])


def final_body(plan, place, field, diagonal, scale, term, keep_p, got, gather_hot, own, other,
               right, dots, more, solution, residual, full):
    q = apply_operator(
        plan, place, field, diagonal, scale, term, keep_p, got, gather_hot, own, other, full
    )
    alpha0 = dots[0:1, :] / dots[1:2, :]
    gamma = more[0:1, :]
    delta = more[1:2, :] - alpha0 * (more[2:3, :] + scale[...] * more[3:4, :])
    beta = gamma / dots[0:1, :]
    alpha = gamma / (delta - beta * gamma / alpha0)
    left = right[...] - alpha0 * field[...]
    w = field[...] - alpha0 * q
    s = w + beta * field[...]
    p = left + beta * right[...]
    solution[...] = alpha0 * right[...] + alpha * p
    residual[...] = left - alpha * s


def local(genotype, allele_freq, right_side, diagonal, mendelian, genomic_weight, send_rows,
          sire_slot, dam_slot):
    blocks = lax.axis_size("snp")
    plan = Plan(genotype, right_side, send_rows)
    rows, cols, half, nb, parts = plan.rows, plan.cols, plan.half, plan.nb, plan.parts
    place = jnp.stack([lax.axis_index("animal"), lax.axis_index("snp") & 1]).astype(I32)
    freq = allele_freq.reshape(1, plan.snps)
    scale = (genomic_weight / (plan.snps * blocks)).reshape(1, cols)
    share = jnp.full((8, cols), 1.0 / blocks, F32)
    weight = mendelian.reshape(1, rows)
    shapes = plan.message_shapes()
    square = ((rows, cols), F32)
    lines = ((8, cols), F32)
    wide = plan.owners * LANES
    work = 2 * rows * cols * plan.snps
    groups = [[0, 1], [2, 3]] if parts == 4 else [list(range(parts))]

    geno, gather_hot, parent_hot, *messages = call(
        lambda *r: begin_body(plan, *r),
        (place, genotype, freq, right_side, send_rows[0], sire_slot.reshape(1, rows),
         dam_slot.reshape(1, rows)),
        (pltpu.VMEM(genotype.shape, BF16), ((rows, wide), BF16), ((wide, rows), BF16), *shapes),
        specs=[HBM] + [VMEM] * 5,
        scratch=[pltpu.VMEM((1, LANES), I32), pltpu.SemaphoreType.DMA((plan.owners,))],
        flops=work,
    )

    def round_trip(field, messages, extra):
        order = plan.bits
        send, keep_e, keep_p = messages[:3]
        left, sources = half, 1
        got = swap(send, "animal", order[0])
        for bit in order[1:]:
            send, keep_e, keep_p = call(
                lambda *r, left=left, sources=sources: merge_body(plan, left, sources, *r),
                (place, got, keep_e, keep_p),
                (plan.tile(left // 2 * nb + half), plan.tile(left // 2 * nb), plan.tile(half)),
            )
            left, sources = left // 2, sources * 2
            got = swap(send, "animal", bit)
        others = []
        for part in range(1, parts):
            send, keep = messages[2 * part + 1 : 2 * part + 3]
            for step, bit in enumerate(plan.orders[part]):
                if step:
                    middle = keep.shape[0] // 2
                    keep, send = keep[:middle], keep[middle:]
                keep = (keep.astype(F32) + swap(send, "animal", bit).astype(F32)).astype(BF16)
            others.append(keep)
        sent, keep_p, term, more = call(
            lambda *r: offspring_body(plan, bool(extra), *r),
            (place, got, keep_e, keep_p, field, parent_hot, weight, *extra),
            (plan.tile(nb + half), plan.tile(half), square, lines if extra else square),
        )
        owned = [sent, *others]
        got = swap(sent, "animal", order[-1])
        held, sources = 1, 1
        for bit in order[-2::-1]:
            sent, keep_p = call(
                lambda *r, held=held, sources=sources: spread_body(plan, held, sources, *r),
                (place, sent, got, keep_p),
                (plan.tile(2 * held * nb + half), plan.tile(half)),
            )
            held, sources = held * 2, sources * 2
            got = swap(sent, "animal", bit)
        pairs = [(sent, got)]
        for part in range(1, parts):
            x = others[part - 1]
            for bit in plan.orders[part][:0:-1]:
                x = jnp.concatenate([x, swap(x, "animal", bit)], axis=0)
            pairs.append((x, swap(x, "animal", plan.orders[part][0])))
        acc = ()
        for index, group in enumerate(groups):
            last = index == len(groups) - 1
            acc = call(
                lambda *r, group=group, first=index == 0, last=last: values_body(
                    plan, group, first, last, *r
                ),
                (place, geno, freq, *[x for part in group for x in pairs[part]], *acc),
                (((rows // 2, cols), F32),) * 2 if last else (square,),
                scratch=[pltpu.VMEM((rows, cols), F32)] if last else [],
                flops=work * len(group) // parts,
            )
        own, other = acc
        value = own + swap(other, "snp", 1)
        bit = 2
        while bit < blocks:
            short = value.astype(BF16)
            value = short.astype(F32) + swap(short, "snp", bit).astype(F32)
            bit *= 2
        return (term, keep_p, got, gather_hot, value, swap(value, "snp", 1)), more, owned

    ends, plain, owned = round_trip(right_side, messages, ())
    full = [pltpu.VMEM((rows, cols), F32)]
    image, dots, *messages = call(
        lambda *r: middle_body(plan, *r),
        (place, right_side, diagonal, scale, *ends, geno, freq),
        (square, lines, *shapes),
        scratch=full,
        flops=work,
    )
    dots = total(dots, "animal")
    before = owned
    ends, more, owned = round_trip(image, messages, (plain, share, diagonal, right_side, dots))
    (more,) = call(
        lambda *r: effect_dots_body(plan, *r), (place, more, dots, *before, *owned), (lines,)
    )
    more = total(total(more, "animal"), "snp")
    return call(
        lambda *r: final_body(plan, *r),
        (place, image, diagonal, scale, *ends, right_side, dots, more),
        (square, square),
        scratch=full,
    )


def solution(mesh):
    placed = (
        P("animal", "snp"),
        P("snp"),
        P("animal", None),
        P("animal", None),
        P("animal"),
        P(),
        P("animal", None, None),
        P("animal"),
        P("animal"),
    )
    return jax.shard_map(
        local,
        mesh=mesh,
        in_specs=placed,
        out_specs=(P("animal", None), P("animal", None)),
        check_vma=False,
    )
```

```python
import jax
import jax.numpy as jnp
from jax import lax
from jax.experimental import pallas as pl
from jax.experimental.pallas import tpu as pltpu
from jax.sharding import PartitionSpec as P


BF16, F32, I32 = jnp.bfloat16, jnp.float32, jnp.int32
LANES = 128
VMEM = pl.BlockSpec(memory_space=pltpu.VMEM)
SMEM = pl.BlockSpec(memory_space=pltpu.SMEM)
HBM = pl.BlockSpec(memory_space=pltpu.HBM)


def call(body, ins, outs, specs=None, limit=24, scratch=(), flops=0,
         placed=True):
    specs = specs or [VMEM] * (len(ins) - 1)
    outs = tuple(o if hasattr(o, "memory_space") else jax.ShapeDtypeStruct(*o) for o in outs)
    moved = sum(a.size * a.dtype.itemsize for a in ins)
    return pl.pallas_call(
        body,
        in_specs=[SMEM, *specs] if placed else [VMEM] * len(ins),
        out_specs=tuple(VMEM for _ in outs),
        out_shape=outs,
        scratch_shapes=scratch,
        cost_estimate=pl.CostEstimate(flops=flops, bytes_accessed=moved, transcendentals=0),
        compiler_params=pltpu.CompilerParams(vmem_limit_bytes=limit << 20),
    )(*ins)


def positions(order):
    if not order:
        return [0]
    rest = positions(order[1:])
    return rest + [j | order[0] for j in rest]


def swap(x, axis, bit):
    size = lax.axis_size(axis)
    return lax.ppermute(x, axis, [(i, i ^ bit) for i in range(size)])


def bits_of(size):
    return [1 << b for b in range(size.bit_length() - 1)]


def part_count(owned):
    return max(1, min(4, owned // LANES))


def colsum(x):
    return jnp.sum(x, axis=0, keepdims=True)


def stack_rows(rows):
    wide = rows[0].shape[1]
    return jnp.concatenate([*rows, jnp.zeros((8 - len(rows), wide), F32)], axis=0)


def split(x):
    high = x.astype(BF16)
    return high, (x - high.astype(F32)).astype(BF16)


def hot_dot(hot, x, dims):
    high, low = split(x)
    dims = (dims, ((), ()))
    out = lax.dot_general(hot, high, dims, preferred_element_type=F32)
    return out + lax.dot_general(hot, low, dims, preferred_element_type=F32)


class Plan:
    def __init__(self, genotype, right_side, send_rows, carry):
        self.owners = lax.axis_size("animal")
        self.rows, self.snps = genotype.shape
        self.cols = right_side.shape[1]
        self.slots = send_rows.shape[2]
        self.half = self.owners // 2
        self.owned = self.snps // self.owners
        self.parts = part_count(self.owned)
        self.width = self.owned // self.parts
        self.nb = self.width // LANES
        bits = bits_of(self.owners)
        flip = [bits[1], bits[0], *bits[2:]]
        self.orders = [bits if part % 2 == 0 else flip for part in range(self.parts)]
        self.bits = bits
        self.sets = [[0, 1], [2, 3]] if self.parts == 4 else [list(range(self.parts))]

        self.groups = lax.axis_size("snp")
        self.kinds = max(1, self.groups // 2)
        self.lane_shift = (self.cols // self.groups).bit_length() - 1
        self.packed = self.slots // self.kinds
        self.pedigree = self.owners * self.packed
        self.carry = carry
        self.line = self.packed + carry

    def tile(self, blocks, slots=0):
        return ((blocks * LANES + slots * self.line, self.cols), BF16)

    def message_shapes(self, group):
        half, nb = self.half, self.nb
        shapes = []
        for part in group:
            if part:
                shapes += [self.tile(half * nb), self.tile(half * nb)]
            else:
                shapes += [self.tile(half * nb, half), self.tile(half * nb), self.tile(0, half)]
        return shapes

    def share(self, group):
        return self.width * len(group)

    def kept_shapes(self, group):
        wide = self.owners * self.share(group)
        return [pltpu.VMEM((self.rows, wide), BF16), ((1, wide), F32)]

    def lane_group(self, shape):
        return lax.broadcasted_iota(I32, shape, 1) >> self.lane_shift

    def fold(self, x):
        shift = self.cols // 2
        while shift >> self.lane_shift:
            x = x + pltpu.roll(x, shift, 1)
            shift //= 2
        return x

    def mine(self, place, x):
        return jnp.where(self.lane_group(x.shape) == place[1], x, 0.0)

    def mix(self, x):
        high = x.astype(BF16).astype(F32)
        return jnp.where(self.lane_group(x.shape) < self.kinds, high, x - high)

    def select(self, pieces):
        kind = self.lane_group(pieces[0].shape) & (self.kinds - 1)
        out = pieces[0]
        for k in range(1, self.kinds):
            out = jnp.where(kind == k, pieces[k], out)
        return out

    def pack(self, x):
        size = self.pedigree
        pieces = [x[k * size : (k + 1) * size] for k in range(self.kinds)]
        return self.select(pieces).astype(BF16)


def encode(plan, rows):
    lines = []
    for row in rows:
        high = row.astype(BF16).astype(F32)
        mid = (row - high).astype(BF16).astype(F32)
        lines += [high, mid, row - high - mid]
    lines.append(jnp.zeros((plan.carry - len(lines), plan.cols), F32))
    return jnp.concatenate(lines, axis=0).astype(BF16)


def decode(total, count):
    return [colsum(total[3 * i : 3 * i + 3]) for i in range(count)]


def put_rows(plan, order, packed, send, offset, keep, sums=None):
    size = plan.packed
    for at, r in enumerate(positions(order)):
        block = packed[r * size : (r + 1) * size]
        out, first = keep, at * plan.line
        if at >= plan.half:
            out, first = send, offset + (at - plan.half) * plan.line
        out[first : first + size] = block
        if sums is not None:
            out[first + size : first + plan.line] = sums


def take_rows(plan, keep_p, got, edge):
    blocks, sums = [], None
    for at in range(plan.owners):
        from_, first = keep_p, at * plan.line
        if at >= plan.half:
            from_, first = got, edge + (at - plan.half) * plan.line
        blocks.append(from_[first : first + plan.packed])
        if plan.carry:
            under = from_[first + plan.packed : first + plan.line].astype(F32)
            sums = under if sums is None else sums + under
    return blocks, sums


def copy_in(plan, group, place, geno, freq, kept, kept_freq, sem, freq_sem):
    wide = plan.share(group)
    copies = []
    for r in range(plan.owners):
        first = (place[0] ^ r) * plan.owned + group[0] * plan.width
        there = pl.ds(pl.multiple_of(first, LANES), wide)
        here = pl.ds(r * wide, wide)
        copies.append((
            pltpu.make_async_copy(freq.at[:, there], kept_freq.at[:, here], freq_sem.at[r]),
            pltpu.make_async_copy(geno.at[:, there], kept.at[:, here], sem.at[r]),
        ))
        for copy in copies[-1]:
            copy.start()
    return copies


def put_effects(plan, group, r, geno, freq, turned, sums, messages):
    wide = plan.share(group)
    here = slice(r * wide, (r + 1) * wide)
    acc = jnp.dot(turned, geno[:, here], preferred_element_type=F32)
    acc = (acc - sums * (2.0 * freq[:, here])).astype(BF16)
    half, nb = plan.half, plan.nb
    messages = list(messages)
    for index, part in enumerate(group):
        send, keep = messages[:2]
        messages = messages[2 if part else 3 :]
        at = positions(plan.orders[part]).index(r)
        out, at = (keep, at) if at < half else (send, at - half)
        for b in range(nb):
            first = index * plan.width + b * LANES
            row = (at * nb + b) * LANES
            out[row : row + LANES] = acc[:, first : first + LANES]


def emit_rows(plan, place, field, gather_hot, messages, sums=None):
    mixed = plan.mix(plan.fold(plan.mine(place, field))).astype(BF16)
    rows = lax.dot_general(
        gather_hot[...], mixed, (((0,), (0,)), ((), ())), preferred_element_type=F32
    )
    offset = plan.half * plan.nb * LANES
    put_rows(plan, plan.bits, plan.pack(rows), messages[0], offset, messages[2], sums)


def turn(field):
    turned = field.T.astype(BF16)
    return turned, jnp.sum(turned.astype(F32), axis=1, keepdims=True)


def turn_out(field, flipped, sums):
    turned, side = turn(field)
    flipped[...] = turned
    sums[...] = jnp.broadcast_to(side, sums.shape)
    return turned, side


def begin_body(plan, place, geno, freq, right_in, send_in, sire_in, dam_in,
               kept, kept_freq, gather_hot, parent_hot, flipped, sums, *rest):
    messages, scratch = rest[:-8], rest[-8:]
    right, send_rows, sire, dam, index, sem, freq_sem, small_sem = scratch
    pairs = ((send_in, send_rows), (sire_in, sire), (dam_in, dam), (right_in, right))
    small = [pltpu.make_async_copy(*pair, small_sem.at[i]) for i, pair in enumerate(pairs)]
    for copy in small:
        copy.start()
    group = plan.sets[0]
    copies = copy_in(plan, group, place, geno, freq, kept, kept_freq, sem, freq_sem)
    me, slots, packed = place[0], plan.slots, plan.packed
    shift, short = slots.bit_length() - 1, packed.bit_length() - 1
    for copy in small[:3]:
        copy.wait()
    for r in range(plan.owners):
        line = send_rows[pl.ds(me ^ r, 1), :]
        for k in range(plan.kinds):
            first = k * plan.pedigree + r * packed
            index[:, first : first + packed] = line[:, k * packed : (k + 1) * packed]

    def spot(slot):
        owner, row = (slot >> shift) ^ me, slot & (slots - 1)
        return (row >> short) * plan.pedigree + (owner << short) + (row & (packed - 1))

    sires, dams = spot(sire[...]), spot(dam[...])
    animal = lax.broadcasted_iota(I32, (plan.rows, LANES), 0)
    row = lax.broadcasted_iota(I32, (LANES, plan.rows), 0)
    for first in range(0, plan.owners * slots, LANES):
        here = slice(first, first + LANES)
        gather_hot[:, here] = jnp.where(animal == index[:, here], 1.0, 0.0).astype(BF16)
        hot = jnp.where(row == sires - first, 1.0, 0.0) + jnp.where(row == dams - first, 1.0, 0.0)
        parent_hot[here, :] = hot.astype(BF16)
    for copy in small[3:]:
        copy.wait()
    emit_rows(plan, place, right[...], gather_hot, messages)
    turned, side = turn_out(right[...], flipped, sums)
    for r in range(plan.owners):
        for copy in copies[r]:
            copy.wait()
        put_effects(plan, group, r, kept, kept_freq, turned, side, messages)


def begin_more_body(plan, group, place, geno, freq, flipped, sums, kept, kept_freq, *rest):
    messages, (sem, freq_sem) = rest[:-2], rest[-2:]
    copies = copy_in(plan, group, place, geno, freq, kept, kept_freq, sem, freq_sem)
    for r in range(plan.owners):
        for copy in copies[r]:
            copy.wait()
        put_effects(plan, group, r, kept, kept_freq, flipped[...], sums[:, :1], messages)


def more_body(plan, group, geno, freq, flipped, sums, *messages):
    for r in range(plan.owners):
        put_effects(plan, group, r, geno, freq, flipped[...], sums[:, :1], messages)


def merge_body(plan, slots_left, sources, got, keep_e, keep_p, send, next_e, next_p):
    half = slots_left // 2
    count = slots_left * plan.nb * LANES
    summed = (keep_e[...].astype(F32) + got[0:count].astype(F32)).astype(BF16)
    next_e[...] = summed[: count // 2]
    send[0 : count // 2] = summed[count // 2 :]
    size, step = half * plan.line, slots_left * plan.line
    for s in range(2 * sources):
        from_, at = (keep_p, s * step) if s < sources else (got, count + (s - sources) * step)
        next_p[s * size : (s + 1) * size] = from_[at : at + size]
        first = count // 2 + s * size
        send[first : first + size] = from_[at + size : at + step]


def add_body(got, keep, *out):
    summed = (keep[...].astype(F32) + got[...].astype(F32)).astype(BF16)
    size = summed.shape[0] // len(out)
    for i, ref in enumerate(out):
        ref[...] = summed[i * size : (i + 1) * size]


def join_body(sent, got, out):
    size = sent.shape[0]
    out[0:size] = sent[...]
    out[size:] = got[...]


def offspring_body(plan, second, place, got, keep_e, keep_p, field, parent_hot, mendelian, *rest):
    if second:
        plain_before, diagonal, right, *rest = rest
    send, keep_back, term, extra = rest
    edge, size = plan.nb * LANES, plan.pedigree
    send[0:edge] = (keep_e[...].astype(F32) + got[0:edge].astype(F32)).astype(BF16)
    blocks, under = take_rows(plan, keep_p, got, edge)
    received = jnp.concatenate(blocks, axis=0)
    pieces = [
        lax.dot_general(
            parent_hot[k * size : (k + 1) * size],
            received,
            (((0,), (0,)), ((), ())),
            preferred_element_type=F32,
        )
        for k in range(plan.kinds)
    ]
    parents = plan.fold(plan.select(pieces))
    weight = jnp.broadcast_to(mendelian[...], (plan.cols, plan.rows)).T
    plain = plan.fold(plan.mine(place, field[...])) - 0.5 * parents
    mendel = weight * plain
    term[...] = mendel
    back = -0.5 * hot_dot(parent_hot[...], mendel, ((1,), (0,)))
    sums = None
    if second:
        gamma, delta = decode(under, 2)
        extra[...] = stack_rows([gamma, delta])
        alpha = gamma / delta
        residual = right[...] - alpha * field[...]
        moved = plain_before[...] - alpha * plain
        sums = encode(plan, [
            colsum(residual * residual),
            colsum(field[...] * residual),
            colsum(diagonal[...] * field[...] * residual),
            plan.mine(place, colsum(mendel * moved)),
        ])
    else:
        extra[...] = plain
    put_rows(plan, plan.bits[::-1], plan.pack(plan.mix(back)), send, edge, keep_back, sums)


def spread_body(plan, slots_held, sources, sent, got, keep_p, send, next_p):
    count = slots_held * plan.nb * LANES
    send[0:count] = sent[0:count]
    send[count : 2 * count] = got[0:count]
    step = plan.half // sources * plan.line
    size = step // 2
    for s in range(2 * sources):
        from_, at = (keep_p, s * step) if s < sources else (got, count + (s - sources) * step)
        next_p[s * size : (s + 1) * size] = from_[at : at + size]
        first = 2 * count + s * size
        send[first : first + size] = from_[at + size : at + step]


def home_rows(plan, place, term, keep_p, got, gather_hot):
    blocks, under = take_rows(plan, keep_p, got, plan.half * plan.nb * LANES)
    order = positions(plan.bits)
    returned = jnp.concatenate([blocks[order.index(r)] for r in range(plan.owners)], axis=0)
    size = plan.pedigree
    pieces = [
        jnp.dot(gather_hot[:, k * size : (k + 1) * size], returned, preferred_element_type=F32)
        for k in range(plan.kinds)
    ]
    return plan.mine(place, term[...] + plan.fold(plan.select(pieces))), under


def lane_total(plan, x):
    side = jnp.sum(x, axis=1, keepdims=True)
    return jnp.broadcast_to(side, (plan.cols, LANES)).T[0:1, :]


def values_body(plan, group, first, last, place, geno, freq, scale, *refs):
    second = plan.carry > 0
    pairs, refs = refs[: 2 * len(group)], refs[2 * len(group) :]
    if second:
        earlier, dots, refs = refs[: 2 * len(group)], refs[2 * len(group)], refs[2 * len(group) + 1 :]
        alpha = dots[0:1, :] / dots[1:2, :]
        alpha = jnp.broadcast_to(alpha, (LANES, plan.cols)).T[:, :1]
    if first:
        term, keep_p, gather_hot, *refs = refs
    elif second:
        before, more_before, *refs = refs
    else:
        before, *refs = refs
    *outs, acc = refs
    turned = (((1,), (1,)), ((), ()))
    nb, half = plan.nb, plan.half

    def block_of(near, far, at):
        held, at = (near, at) if at < half else (far, at - half)
        tiles = [held[(at * nb + b) * LANES : (at * nb + b + 1) * LANES] for b in range(nb)]
        return jnp.concatenate(tiles, axis=1)

    spread, inner = None, None
    for index, part in enumerate(group):
        near, far = pairs[2 * index : 2 * index + 2]
        for at, r in enumerate(positions(plan.orders[part])):
            first_column = r * plan.share(group) + index * plan.width
            here = slice(first_column, first_column + plan.width)
            block = block_of(near, far, at)
            wide = block.astype(F32)
            off = wide * (2.0 * freq[:, here])
            if second:
                old = block_of(*earlier[2 * index : 2 * index + 2], at).astype(F32)
                product = wide * (old - alpha * wide)
                inner = product if inner is None else inner + product
            value = lax.dot_general(geno[:, here], block, turned, preferred_element_type=F32)
            if spread is None:
                spread, acc[...] = off, value
            else:
                spread = spread + off
                acc[...] += value
    shift = lane_total(plan, spread)
    if first:
        base, under = home_rows(plan, place, term, keep_p, pairs[1], gather_hot)
    else:
        base = before[...]
    if second:
        inner = scale[...] * lane_total(plan, inner)
        if first:
            gamma, cross, own_part, pedigree = decode(under, 4)
            inner = inner + pedigree
            outs[-1][...] = stack_rows([gamma, cross, own_part, inner])
        else:
            inner = inner + more_before[3:4, :]
    if last:
        acc[...] = base + scale[...] * (acc[...] - shift)
        own, other = outs[:2]
        rows = plan.rows // 2
        at = (place[1] & 1) * rows
        own[0:rows] = acc[pl.ds(pl.multiple_of(at, rows), rows), :]
        other[0:rows] = acc[pl.ds(pl.multiple_of(rows - at, rows), rows), :]
        if second:
            own[rows:] = stack_rows([inner])
            other[rows:] = stack_rows([inner])
    else:
        outs[0][...] = base + scale[...] * (acc[...] - shift)


def apply_operator(place, field, diagonal, own, other, full):
    rows = field.shape[0] // 2
    at = (place[1] & 1) * rows
    full[pl.ds(pl.multiple_of(at, rows), rows), :] = own[0:rows]
    full[pl.ds(pl.multiple_of(rows - at, rows), rows), :] = other[0:rows]
    return diagonal[...] * field[...] + full[...]


def middle_body(plan, place, field, diagonal, own, other, geno, freq, gather_hot,
                image, flipped, sums, *rest):
    messages, full = rest[:-1], rest[-1]
    out = apply_operator(place, field, diagonal, own, other, full)
    image[...] = out
    dots = encode(plan, [colsum(field[...] * field[...]), colsum(out * field[...])])
    emit_rows(plan, place, image[...], gather_hot, messages, dots)
    turned, side = turn_out(image[...], flipped, sums)
    for r in range(plan.owners):
        put_effects(plan, plan.sets[0], r, geno, freq, turned, side, messages)


def final_body(place, field, diagonal, own, other, right, dots, more,
               solution, residual, full):
    q = apply_operator(place, field, diagonal, own, other, full)
    alpha0 = dots[0:1, :] / dots[1:2, :]
    gamma = more[0:1, :]
    rows = field.shape[0] // 2
    delta = more[1:2, :] - alpha0 * (more[2:3, :] + own[rows : rows + 1, :])
    beta = gamma / dots[0:1, :]
    alpha = gamma / (delta - beta * gamma / alpha0)
    left = right[...] - alpha0 * field[...]
    w = field[...] - alpha0 * q
    s = w + beta * field[...]
    p = left + beta * right[...]
    solution[...] = alpha0 * right[...] + alpha * p
    residual[...] = left - alpha * s


def local(genotype, allele_freq, right_side, diagonal, mendelian, genomic_weight, send_rows,
          sire_slot, dam_slot):
    blocks = lax.axis_size("snp")
    plan = Plan(genotype, right_side, send_rows, 0)
    summing = Plan(genotype, right_side, send_rows, 16)
    rows, cols, half, nb, parts = plan.rows, plan.cols, plan.half, plan.nb, plan.parts
    place = jnp.stack([lax.axis_index("animal"), lax.axis_index("snp")]).astype(I32)
    freq = allele_freq.reshape(1, plan.snps)
    scale = (genomic_weight / (plan.snps * blocks)).reshape(1, cols)
    weight = mendelian.reshape(1, rows)
    square = ((rows, cols), F32)
    lines = ((8, cols), F32)
    wide = plan.owners * plan.slots
    work = 2 * rows * cols * plan.snps
    groups = plan.sets
    turned = (((cols, rows), BF16), ((cols, LANES), F32))
    full = [pltpu.VMEM((rows, cols), F32)]

    whole, frequency = (
        pltpu.with_memory_space_constraint(x, pltpu.HBM) for x in (genotype, freq)
    )
    copies = [pltpu.SemaphoreType.DMA((plan.owners,))] * 2
    geno, freq, gather_hot, parent_hot, flipped, sums, *messages = call(
        lambda *r: begin_body(plan, *r),
        (place, whole, frequency, *[
            pltpu.with_memory_space_constraint(x, pltpu.HBM)
            for x in (right_side, send_rows[0], sire_slot.reshape(1, rows),
                      dam_slot.reshape(1, rows))
        ]),
        (*plan.kept_shapes(groups[0]), ((rows, wide), BF16), ((wide, rows), BF16), *turned,
         *plan.message_shapes(groups[0])),
        specs=[HBM] * 6,
        scratch=[
            pltpu.VMEM((rows, cols), F32),
            pltpu.VMEM(send_rows.shape[1:], I32),
            pltpu.VMEM((1, rows), I32),
            pltpu.VMEM((1, rows), I32),
            pltpu.VMEM((1, wide), I32),
            *copies,
            pltpu.SemaphoreType.DMA((4,)),
        ],
        flops=work,
    )
    kept = [(geno, freq)]
    for group in groups[1:]:
        *pair, = call(
            lambda *r, group=group: begin_more_body(plan, group, *r),
            (place, whole, frequency, flipped, sums),
            (*plan.kept_shapes(group), *plan.message_shapes(group)),
            specs=[HBM] * 2 + [VMEM] * 2,
            scratch=copies,
            flops=work,
        )
        kept.append(tuple(pair[:2]))
        messages += pair[2:]

    def round_trip(op, plan, field, messages, extra, earlier):
        order = plan.bits
        send, keep_e, keep_p = messages[:3]
        left, sources = half, 1
        got = swap(send, "animal", order[0])
        for bit in order[1:]:
            send, keep_e, keep_p = call(
                lambda *r, left=left, sources=sources: merge_body(plan, left, sources, *r),
                (got, keep_e, keep_p),
                (plan.tile(left // 2 * nb, half), plan.tile(left // 2 * nb), plan.tile(0, half)),
                placed=False,
            )
            left, sources = left // 2, sources * 2
            got = swap(send, "animal", bit)
        others = []
        for part in range(1, parts):
            other, keep = messages[2 * part + 1 : 2 * part + 3]
            for i, bit in enumerate(plan.orders[part]):
                got_e = swap(other, "animal", bit)
                size = half >> i
                outs = (plan.tile(size // 2 * nb),) * 2 if size > 1 else (plan.tile(nb),)
                keep, *other = call(add_body, (got_e, keep), outs, placed=False)
                other = other[0] if other else None
            others.append(keep)
        sent, keep_p, term, more = call(
            lambda *r: offspring_body(plan, bool(extra), *r),
            (place, got, keep_e, keep_p, field, parent_hot, weight, *extra),
            (plan.tile(nb, half), plan.tile(0, half), square, lines if extra else square),
        )
        got = swap(sent, "animal", order[-1])
        held, sources = 1, 1
        for bit in order[-2::-1]:
            sent, keep_p = call(
                lambda *r, held=held, sources=sources: spread_body(plan, held, sources, *r),
                (sent, got, keep_p),
                (plan.tile(2 * held * nb, half), plan.tile(0, half)),
                placed=False,
            )
            held, sources = held * 2, sources * 2
            got = swap(sent, "animal", bit)
        pairs = [(sent, got)]
        for part in range(1, parts):
            x = others[part - 1]
            for step, bit in enumerate(plan.orders[part][::-1]):
                got_e = swap(x, "animal", bit)
                if bit == plan.orders[part][0]:
                    pairs.append((x, got_e))
                else:
                    outs = (plan.tile(2 * nb << step),)
                    (x,) = call(join_body, (x, got_e), outs, placed=False)
        acc = (term, keep_p, gather_hot)
        tail = ((rows // 2 + (8 if op else 0), cols), F32)
        for index, group in enumerate(groups):
            first, last = index == 0, index == len(groups) - 1
            mine = [x for part in group for x in pairs[part]]
            if op:
                mine += [*(x for part in group for x in earlier[part]), more]
            outs = [tail, tail] if last else [square]
            if op and first:
                outs.append(lines)
            acc = call(
                lambda *r, group=group, first=first, last=last: values_body(
                    plan, group, first, last, *r
                ),
                (place, *kept[index], scale, *mine, *acc),
                outs,
                scratch=full,
                flops=work * len(group) // parts,
            )
            if op and first:
                sums = acc[-1]
                acc = acc if not last else acc[:-1]
        own, other = acc
        value = own + swap(other, "snp", 1)
        for bit in bits_of(blocks)[1:]:
            value = value + swap(value, "snp", bit)
        after = (more, sums) if op else (more, pairs)
        return value, swap(value, "snp", 1), *after

    own, other, plain, earlier = round_trip(0, plan, right_side, messages, (), None)
    image, flipped, sums, *messages = call(
        lambda *r: middle_body(summing, *r),
        (place, right_side, diagonal, own, other, *kept[0], gather_hot),
        (square, *turned, *summing.message_shapes(groups[0])),
        scratch=full,
        flops=work,
    )
    for index, group in enumerate(groups[1:]):
        messages += call(
            lambda *r, group=group: more_body(plan, group, *r),
            (*kept[index + 1], flipped, sums),
            plan.message_shapes(group),
            flops=work,
            placed=False,
        )
    own, other, dots, more = round_trip(
        1, summing, image, messages, (plain, diagonal, right_side), earlier
    )
    return call(
        final_body,
        (place, image, diagonal, own, other, right_side, dots, more),
        (square, square),
        scratch=full,
    )


def solution(mesh):
    placed = (
        P("animal", "snp"),
        P("snp"),
        P("animal", None),
        P("animal", None),
        P("animal"),
        P(),
        P("animal", None, None),
        P("animal"),
        P("animal"),
    )

    return jax.shard_map(
        local,
        mesh=mesh,
        in_specs=placed,
        out_specs=(P("animal", None), P("animal", None)),
        check_vma=False,
    )
```

```python
import jax
import jax.numpy as jnp
from jax import lax
from jax.experimental import pallas as pl
from jax.experimental.pallas import tpu as pltpu
from jax.sharding import PartitionSpec as P


BF16, F32, I32 = jnp.bfloat16, jnp.float32, jnp.int32
LANES = 128
VMEM = pl.BlockSpec(memory_space=pltpu.VMEM)
SMEM = pl.BlockSpec(memory_space=pltpu.SMEM)
HBM = pl.BlockSpec(memory_space=pltpu.HBM)


def call(body, ins, outs, specs=None, limit=24, scratch=(), flops=0,
         placed=True):
    specs = specs or [VMEM] * (len(ins) - 1)
    outs = tuple(o if hasattr(o, "memory_space") else jax.ShapeDtypeStruct(*o) for o in outs)
    moved = sum(a.size * a.dtype.itemsize for a in ins)
    return pl.pallas_call(
        body,
        in_specs=[SMEM, *specs] if placed else [VMEM] * len(ins),
        out_specs=tuple(VMEM for _ in outs),
        out_shape=outs,
        scratch_shapes=scratch,
        cost_estimate=pl.CostEstimate(flops=flops, bytes_accessed=moved, transcendentals=0),
        compiler_params=pltpu.CompilerParams(vmem_limit_bytes=limit << 20),
    )(*ins)


def positions(order):
    if not order:
        return [0]
    rest = positions(order[1:])
    return rest + [j | order[0] for j in rest]


def swap(x, axis, bit):
    size = lax.axis_size(axis)
    return lax.ppermute(x, axis, [(i, i ^ bit) for i in range(size)])


def bits_of(size):
    return [1 << b for b in range(size.bit_length() - 1)]


def part_count(owned):
    return max(1, min(4, owned // LANES))


def colsum(x):
    return jnp.sum(x, axis=0, keepdims=True)


def stack_rows(rows):
    wide = rows[0].shape[1]
    return jnp.concatenate([*rows, jnp.zeros((8 - len(rows), wide), F32)], axis=0)


def split(x):
    high = x.astype(BF16)
    return high, (x - high.astype(F32)).astype(BF16)


def hot_dot(hot, x, dims):
    high, low = split(x)
    dims = (dims, ((), ()))
    out = lax.dot_general(hot, high, dims, preferred_element_type=F32)
    return out + lax.dot_general(hot, low, dims, preferred_element_type=F32)


class Plan:
    def __init__(self, genotype, right_side, send_rows, carry):
        self.owners = lax.axis_size("animal")
        self.rows, self.snps = genotype.shape
        self.cols = right_side.shape[1]
        self.slots = send_rows.shape[2]
        self.half = self.owners // 2
        self.owned = self.snps // self.owners
        self.parts = part_count(self.owned)
        self.width = self.owned // self.parts
        self.nb = self.width // LANES
        bits = bits_of(self.owners)
        flip = [bits[1], bits[0], *bits[2:]]
        early = [bits[0], *bits[2:], bits[1]]
        self.orders = [bits, flip, early, flip][: self.parts]
        self.bits = bits
        self.sets = [[0, 1], [2, 3]] if self.parts == 4 else [list(range(self.parts))]

        self.groups = lax.axis_size("snp")
        self.kinds = max(1, self.groups // 2)
        self.lane_shift = (self.cols // self.groups).bit_length() - 1
        self.packed = self.slots // self.kinds
        self.pedigree = self.owners * self.packed
        self.carry = carry
        self.line = self.packed + carry

    def tile(self, blocks, slots=0):
        return ((blocks * LANES + slots * self.line, self.cols), BF16)

    def message_shapes(self, group):
        half, nb = self.half, self.nb
        shapes = []
        for part in group:
            if part:
                shapes += [self.tile(half * nb), self.tile(half * nb)]
            else:
                shapes += [self.tile(half * nb, half), self.tile(half * nb), self.tile(0, half)]
        return shapes

    def share(self, group):
        return self.width * len(group)

    def kept_shapes(self, group):
        wide = self.owners * self.share(group)
        return [pltpu.VMEM((self.rows, wide), BF16), ((1, wide), F32)]

    def lane_group(self, shape):
        return lax.broadcasted_iota(I32, shape, 1) >> self.lane_shift

    def fold(self, x):
        shift = self.cols // 2
        while shift >> self.lane_shift:
            x = x + pltpu.roll(x, shift, 1)
            shift //= 2
        return x

    def mine(self, place, x):
        return jnp.where(self.lane_group(x.shape) == place[1], x, 0.0)

    def mix(self, x):
        high = x.astype(BF16).astype(F32)
        return jnp.where(self.lane_group(x.shape) < self.kinds, high, x - high)

    def select(self, pieces):
        kind = self.lane_group(pieces[0].shape) & (self.kinds - 1)
        out = pieces[0]
        for k in range(1, self.kinds):
            out = jnp.where(kind == k, pieces[k], out)
        return out

    def pack(self, x):
        size = self.pedigree
        pieces = [x[k * size : (k + 1) * size] for k in range(self.kinds)]
        return self.select(pieces).astype(BF16)


def encode(plan, rows):
    lines = []
    for row in rows:
        high = row.astype(BF16).astype(F32)
        mid = (row - high).astype(BF16).astype(F32)
        lines += [high, mid, row - high - mid]
    lines.append(jnp.zeros((plan.carry - len(lines), plan.cols), F32))
    return jnp.concatenate(lines, axis=0).astype(BF16)


def decode(total, count):
    return [colsum(total[3 * i : 3 * i + 3]) for i in range(count)]


def put_rows(plan, order, packed, send, offset, keep, sums=None):
    size = plan.packed
    for at, r in enumerate(positions(order)):
        block = packed[r * size : (r + 1) * size]
        out, first = keep, at * plan.line
        if at >= plan.half:
            out, first = send, offset + (at - plan.half) * plan.line
        out[first : first + size] = block
        if sums is not None:
            out[first + size : first + plan.line] = sums


def take_rows(plan, keep_p, got, edge):
    blocks, sums = [], None
    for at in range(plan.owners):
        from_, first = keep_p, at * plan.line
        if at >= plan.half:
            from_, first = got, edge + (at - plan.half) * plan.line
        blocks.append(from_[first : first + plan.packed])
        if plan.carry:
            under = from_[first + plan.packed : first + plan.line].astype(F32)
            sums = under if sums is None else sums + under
    return blocks, sums


def copy_in(plan, group, place, geno, freq, kept, kept_freq, sem, freq_sem):
    wide = plan.share(group)
    copies = []
    for r in range(plan.owners):
        first = (place[0] ^ r) * plan.owned + group[0] * plan.width
        there = pl.ds(pl.multiple_of(first, LANES), wide)
        here = pl.ds(r * wide, wide)
        copies.append((
            pltpu.make_async_copy(freq.at[:, there], kept_freq.at[:, here], freq_sem.at[r]),
            pltpu.make_async_copy(geno.at[:, there], kept.at[:, here], sem.at[r]),
        ))
        for copy in copies[-1]:
            copy.start()
    return copies


def put_effects(plan, group, r, geno, freq, turned, sums, messages):
    wide = plan.share(group)
    here = slice(r * wide, (r + 1) * wide)
    acc = jnp.dot(turned, geno[:, here], preferred_element_type=F32)
    acc = (acc - sums * (2.0 * freq[:, here])).astype(BF16)
    half, nb = plan.half, plan.nb
    messages = list(messages)
    for index, part in enumerate(group):
        send, keep = messages[:2]
        messages = messages[2 if part else 3 :]
        at = positions(plan.orders[part]).index(r)
        out, at = (keep, at) if at < half else (send, at - half)
        for b in range(nb):
            first = index * plan.width + b * LANES
            row = (at * nb + b) * LANES
            out[row : row + LANES] = acc[:, first : first + LANES]


def emit_rows(plan, place, field, gather_turned, messages, sums=None):
    mixed = plan.mix(plan.fold(plan.mine(place, field))).astype(BF16)
    rows = jnp.dot(gather_turned[...], mixed, preferred_element_type=F32)
    offset = plan.half * plan.nb * LANES
    put_rows(plan, plan.bits, plan.pack(rows), messages[0], offset, messages[2], sums)


def turn(field):
    turned = field.T.astype(BF16)
    return turned, jnp.sum(turned.astype(F32), axis=1, keepdims=True)


def fill_index(plan, place, send_rows, index):
    packed = plan.packed
    for r in range(plan.owners):
        line = send_rows[pl.ds(place[0] ^ r, 1), :]
        for k in range(plan.kinds):
            first = k * plan.pedigree + r * packed
            index[:, first : first + packed] = line[:, k * packed : (k + 1) * packed]


def turn_out(field, flipped, sums):
    turned, side = turn(field)
    flipped[...] = turned
    sums[...] = jnp.broadcast_to(side, sums.shape)
    return turned, side


def begin_body(plan, place, geno, freq, right_in, send_in,
               kept, kept_freq, gather_turned, flipped, sums, *rest):
    messages, scratch = rest[:-6], rest[-6:]
    right, send_rows, index, sem, freq_sem, small_sem = scratch
    pairs = ((send_in, send_rows), (right_in, right))
    small = [pltpu.make_async_copy(*pair, small_sem.at[i]) for i, pair in enumerate(pairs)]
    for copy in small:
        copy.start()
    group = plan.sets[0]
    copies = copy_in(plan, group, place, geno, freq, kept, kept_freq, sem, freq_sem)
    small[0].wait()
    fill_index(plan, place, send_rows, index)
    tall = jnp.broadcast_to(index[...].astype(F32), (LANES, index.shape[1])).T
    lane = lax.broadcasted_iota(I32, tall.shape, 1).astype(F32)
    for first in range(0, plan.rows, LANES):
        hot = jnp.where(lane + first == tall, 1.0, 0.0)
        gather_turned[:, first : first + LANES] = hot.astype(BF16)
    small[1].wait()
    emit_rows(plan, place, right[...], gather_turned, messages)
    turned, side = turn_out(right[...], flipped, sums)
    for r in range(plan.owners):
        for copy in copies[r]:
            copy.wait()
        put_effects(plan, group, r, kept, kept_freq, turned, side, messages)


def tables_body(plan, place, sire, dam, mendelian, send_rows, parent_hot, parent_turned, weight,
                gather_hot, index):
    me, slots, packed = place[0], plan.slots, plan.packed
    shift, short = slots.bit_length() - 1, packed.bit_length() - 1

    def spot(slot):
        owner, row = (slot >> shift) ^ me, slot & (slots - 1)
        return (row >> short) * plan.pedigree + (owner << short) + (row & (packed - 1))

    def column(line):
        return jnp.broadcast_to(line, (LANES, plan.rows)).T

    sires, dams = spot(sire[...]), spot(dam[...])
    tall = [column(x.astype(F32)) for x in (sires, dams)]
    weight[...] = column(mendelian[...])
    fill_index(plan, place, send_rows, index)
    animal = lax.broadcasted_iota(I32, (plan.rows, LANES), 0)
    row = lax.broadcasted_iota(I32, (LANES, plan.rows), 0)
    lane = lax.broadcasted_iota(I32, (plan.rows, LANES), 1).astype(F32)
    for first in range(0, plan.owners * slots, LANES):
        here = slice(first, first + LANES)
        hot = jnp.where(row == sires - first, 1.0, 0.0) + jnp.where(row == dams - first, 1.0, 0.0)
        parent_hot[here, :] = hot.astype(BF16)
        hot = jnp.where(lane + first == tall[0], 1.0, 0.0)
        hot = hot + jnp.where(lane + first == tall[1], 1.0, 0.0)
        parent_turned[:, here] = hot.astype(BF16)
        gather_hot[:, here] = jnp.where(animal == index[:, here], 1.0, 0.0).astype(BF16)


def begin_more_body(plan, group, place, geno, freq, flipped, sums, kept, kept_freq, *rest):
    messages, (sem, freq_sem) = rest[:-2], rest[-2:]
    copies = copy_in(plan, group, place, geno, freq, kept, kept_freq, sem, freq_sem)
    for r in range(plan.owners):
        for copy in copies[r]:
            copy.wait()
        put_effects(plan, group, r, kept, kept_freq, flipped[...], sums[:, :1], messages)


def more_body(plan, group, geno, freq, flipped, sums, *messages):
    for r in range(plan.owners):
        put_effects(plan, group, r, geno, freq, flipped[...], sums[:, :1], messages)


def merge_body(plan, slots_left, sources, got, keep_e, keep_p, send, next_e, next_p):
    half = slots_left // 2
    count = slots_left * plan.nb * LANES
    summed = (keep_e[...].astype(F32) + got[0:count].astype(F32)).astype(BF16)
    next_e[...] = summed[: count // 2]
    send[0 : count // 2] = summed[count // 2 :]
    size, step = half * plan.line, slots_left * plan.line
    for s in range(2 * sources):
        from_, at = (keep_p, s * step) if s < sources else (got, count + (s - sources) * step)
        next_p[s * size : (s + 1) * size] = from_[at : at + size]
        first = count // 2 + s * size
        send[first : first + size] = from_[at + size : at + step]


def add_body(got, keep, *out):
    summed = (keep[...].astype(F32) + got[...].astype(F32)).astype(BF16)
    size = summed.shape[0] // len(out)
    for i, ref in enumerate(out):
        ref[...] = summed[i * size : (i + 1) * size]


def join_body(sent, got, out):
    size = sent.shape[0]
    out[0:size] = sent[...]
    out[size:] = got[...]


def offspring_body(plan, second, place, got, keep_e, keep_p, field, parent_hot, parent_turned,
                   weight, *rest):
    if second:
        plain_before, diagonal, right, *rest = rest
    send, keep_back, term, extra = rest
    edge, size = plan.nb * LANES, plan.pedigree
    send[0:edge] = (keep_e[...].astype(F32) + got[0:edge].astype(F32)).astype(BF16)
    blocks, under = take_rows(plan, keep_p, got, edge)
    received = jnp.concatenate(blocks, axis=0)
    pieces = [
        jnp.dot(parent_turned[:, k * size : (k + 1) * size], received, preferred_element_type=F32)
        for k in range(plan.kinds)
    ]
    parents = plan.fold(plan.select(pieces))
    plain = plan.fold(plan.mine(place, field[...])) - 0.5 * parents
    mendel = weight[...] * plain
    term[...] = mendel
    back = -0.5 * hot_dot(parent_hot[...], mendel, ((1,), (0,)))
    sums = None
    if second:
        gamma, delta = decode(under, 2)
        extra[...] = stack_rows([gamma, delta])
        alpha = gamma / delta
        residual = right[...] - alpha * field[...]
        moved = plain_before[...] - alpha * plain
        sums = encode(plan, [
            colsum(residual * residual),
            colsum(field[...] * residual),
            colsum(diagonal[...] * field[...] * residual),
            plan.mine(place, colsum(mendel * moved)),
        ])
    else:
        extra[...] = plain
    put_rows(plan, plan.bits[::-1], plan.pack(plan.mix(back)), send, edge, keep_back, sums)


def spread_body(plan, slots_held, sources, sent, got, keep_p, send, next_p):
    count = slots_held * plan.nb * LANES
    send[0:count] = sent[0:count]
    send[count : 2 * count] = got[0:count]
    step = plan.half // sources * plan.line
    size = step // 2
    for s in range(2 * sources):
        from_, at = (keep_p, s * step) if s < sources else (got, count + (s - sources) * step)
        next_p[s * size : (s + 1) * size] = from_[at : at + size]
        first = 2 * count + s * size
        send[first : first + size] = from_[at + size : at + step]


def home_rows(plan, place, term, keep_p, got, gather_hot):
    blocks, under = take_rows(plan, keep_p, got, plan.half * plan.nb * LANES)
    order = positions(plan.bits)
    returned = jnp.concatenate([blocks[order.index(r)] for r in range(plan.owners)], axis=0)
    size = plan.pedigree
    pieces = [
        jnp.dot(gather_hot[:, k * size : (k + 1) * size], returned, preferred_element_type=F32)
        for k in range(plan.kinds)
    ]
    return plan.mine(place, term[...] + plan.fold(plan.select(pieces))), under


def lane_total(plan, x):
    side = jnp.sum(x, axis=1, keepdims=True)
    return jnp.broadcast_to(side, (plan.cols, LANES)).T[0:1, :]


def values_body(plan, far, place, *refs):
    second = plan.carry > 0
    kept, refs = refs[: 2 * len(plan.sets)], refs[2 * len(plan.sets) :]
    scale, refs = refs[0], refs[1:]
    held, refs = refs[: plan.parts], refs[plan.parts :]
    if second:
        earlier, dots, refs = refs[: plan.parts], refs[plan.parts], refs[plan.parts + 1 :]
        alpha = dots[0:1, :] / dots[1:2, :]
        alpha = jnp.broadcast_to(alpha, (LANES, plan.cols)).T[:, :1]
    if far:
        before, refs = refs[0], refs[1:]
        if second:
            inner_before, refs = refs[0], refs[1:]
        term, keep_p, gather_hot, *refs = refs
    *outs, acc = refs
    turned = (((1,), (1,)), ((), ()))
    nb, half = plan.nb, plan.half

    def block_of(ref, at):
        tiles = [ref[(at * nb + b) * LANES : (at * nb + b + 1) * LANES] for b in range(nb)]
        return jnp.concatenate(tiles, axis=1)

    spread, inner = None, None
    for number, group in enumerate(plan.sets):
        geno, freq = kept[2 * number : 2 * number + 2]
        for index, part in enumerate(group):
            order = positions(plan.orders[part])
            for at, r in enumerate(order[half:] if far else order[:half]):
                first_column = r * plan.share(group) + index * plan.width
                here = slice(first_column, first_column + plan.width)
                block = block_of(held[part], at)
                wide = block.astype(F32)
                off = wide * (2.0 * freq[:, here])
                if second:
                    product = wide * (block_of(earlier[part], at).astype(F32) - alpha * wide)
                    inner = product if inner is None else inner + product
                value = lax.dot_general(
                    geno[:, here], block, turned, preferred_element_type=F32
                )
                if spread is None:
                    spread, acc[...] = off, value
                else:
                    spread = spread + off
                    acc[...] += value
    values = scale[...] * (acc[...] - lane_total(plan, spread))
    if second:
        inner = scale[...] * lane_total(plan, inner)
    if not far:
        outs[0][...] = values
        if second:
            outs[1][...] = stack_rows([inner])
        return
    home, under = home_rows(plan, place, term, keep_p, held[0], gather_hot)
    acc[...] = before[...] + values + home
    own, other = outs[:2]
    rows = plan.rows // 2
    at = (place[1] & 1) * rows
    own[0:rows] = acc[pl.ds(pl.multiple_of(at, rows), rows), :]
    other[0:rows] = acc[pl.ds(pl.multiple_of(rows - at, rows), rows), :]
    if second:
        gamma, cross, own_part, pedigree = decode(under, 4)
        outs[2][...] = stack_rows([gamma, cross, own_part])
        inner = inner + inner_before[0:1, :] + pedigree
        own[rows:] = stack_rows([inner])
        other[rows:] = stack_rows([inner])


def apply_operator(place, field, diagonal, own, other, full):
    rows = field.shape[0] // 2
    at = (place[1] & 1) * rows
    full[pl.ds(pl.multiple_of(at, rows), rows), :] = own[0:rows]
    full[pl.ds(pl.multiple_of(rows - at, rows), rows), :] = other[0:rows]
    return diagonal[...] * field[...] + full[...]


def middle_body(plan, place, field, diagonal, own, other, geno, freq, gather_turned,
                image, flipped, sums, *rest):
    messages, full = rest[:-1], rest[-1]
    out = apply_operator(place, field, diagonal, own, other, full)
    image[...] = out
    dots = encode(plan, [colsum(field[...] * field[...]), colsum(out * field[...])])
    emit_rows(plan, place, image[...], gather_turned, messages, dots)
    turned, side = turn_out(image[...], flipped, sums)
    for r in range(plan.owners):
        put_effects(plan, plan.sets[0], r, geno, freq, turned, side, messages)


def final_body(place, field, diagonal, own, other, right, dots, more,
               solution, residual, full):
    q = apply_operator(place, field, diagonal, own, other, full)
    alpha0 = dots[0:1, :] / dots[1:2, :]
    gamma = more[0:1, :]
    rows = field.shape[0] // 2
    delta = more[1:2, :] - alpha0 * (more[2:3, :] + own[rows : rows + 1, :])
    beta = gamma / dots[0:1, :]
    alpha = gamma / (delta - beta * gamma / alpha0)
    left = right[...] - alpha0 * field[...]
    w = field[...] - alpha0 * q
    s = w + beta * field[...]
    p = left + beta * right[...]
    solution[...] = alpha0 * right[...] + alpha * p
    residual[...] = left - alpha * s


def local(genotype, allele_freq, right_side, diagonal, mendelian, genomic_weight, send_rows,
          sire_slot, dam_slot):
    blocks = lax.axis_size("snp")
    plan = Plan(genotype, right_side, send_rows, 0)
    summing = Plan(genotype, right_side, send_rows, 16)
    rows, cols, half, nb, parts = plan.rows, plan.cols, plan.half, plan.nb, plan.parts
    place = jnp.stack([lax.axis_index("animal"), lax.axis_index("snp")]).astype(I32)
    freq = allele_freq.reshape(1, plan.snps)
    scale = (genomic_weight / (plan.snps * blocks)).reshape(1, cols)
    square = ((rows, cols), F32)
    lines = ((8, cols), F32)
    wide = plan.owners * plan.slots
    work = 2 * rows * cols * plan.snps
    groups = plan.sets
    turned = (((cols, rows), BF16), ((cols, LANES), F32))
    full = [pltpu.VMEM((rows, cols), F32)]

    whole, frequency = (
        pltpu.with_memory_space_constraint(x, pltpu.HBM) for x in (genotype, freq)
    )
    copies = [pltpu.SemaphoreType.DMA((plan.owners,))] * 2
    geno, freq, gather_turned, flipped, sums, *messages = call(
        lambda *r: begin_body(plan, *r),
        (place, whole, frequency, *[
            pltpu.with_memory_space_constraint(x, pltpu.HBM)
            for x in (right_side, send_rows[0])
        ]),
        (*plan.kept_shapes(groups[0]), ((wide, rows), BF16), *turned,
         *plan.message_shapes(groups[0])),
        specs=[HBM] * 4,
        scratch=[
            pltpu.VMEM((rows, cols), F32),
            pltpu.VMEM(send_rows.shape[1:], I32),
            pltpu.VMEM((1, wide), I32),
            *copies,
            pltpu.SemaphoreType.DMA((2,)),
        ],
        flops=work,
    )
    *tables, gather_hot = call(
        lambda *r: tables_body(plan, *r),
        (place, sire_slot.reshape(1, rows), dam_slot.reshape(1, rows), mendelian.reshape(1, rows),
         send_rows[0]),
        (((wide, rows), BF16), ((rows, wide), BF16), square, ((rows, wide), BF16)),
        scratch=[pltpu.VMEM((1, wide), I32)],
    )
    kept = [(geno, freq)]
    for group in groups[1:]:
        *pair, = call(
            lambda *r, group=group: begin_more_body(plan, group, *r),
            (place, whole, frequency, flipped, sums),
            (*plan.kept_shapes(group), *plan.message_shapes(group)),
            specs=[HBM] * 2 + [VMEM] * 2,
            scratch=copies,
            flops=work,
        )
        kept.append(tuple(pair[:2]))
        messages += pair[2:]

    def round_trip(op, plan, field, messages, extra, earlier):
        order = plan.bits
        send, keep_e, keep_p = messages[:3]
        left, sources = half, 1
        got = swap(send, "animal", order[0])
        for bit in order[1:]:
            send, keep_e, keep_p = call(
                lambda *r, left=left, sources=sources: merge_body(plan, left, sources, *r),
                (got, keep_e, keep_p),
                (plan.tile(left // 2 * nb, half), plan.tile(left // 2 * nb), plan.tile(0, half)),
                placed=False,
            )
            left, sources = left // 2, sources * 2
            got = swap(send, "animal", bit)
        others = []
        for part in range(1, parts):
            other, keep = messages[2 * part + 1 : 2 * part + 3]
            for i, bit in enumerate(plan.orders[part]):
                got_e = swap(other, "animal", bit)
                size = half >> i
                outs = (plan.tile(size // 2 * nb),) * 2 if size > 1 else (plan.tile(nb),)
                keep, *other = call(add_body, (got_e, keep), outs, placed=False)
                other = other[0] if other else None
            others.append(keep)
        sent, keep_p, term, more = call(
            lambda *r: offspring_body(plan, bool(extra), *r),
            (place, got, keep_e, keep_p, field, *tables, *extra),
            (plan.tile(nb, half), plan.tile(0, half), square, lines if extra else square),
        )
        got = swap(sent, "animal", order[-1])
        held, sources = 1, 1
        for bit in order[-2::-1]:
            sent, keep_p = call(
                lambda *r, held=held, sources=sources: spread_body(plan, held, sources, *r),
                (sent, got, keep_p),
                (plan.tile(2 * held * nb, half), plan.tile(0, half)),
                placed=False,
            )
            held, sources = held * 2, sources * 2
            got = swap(sent, "animal", bit)
        pairs = [(sent, got)]
        for part in range(1, parts):
            x = others[part - 1]
            for step, bit in enumerate(plan.orders[part][::-1]):
                got_e = swap(x, "animal", bit)
                if bit == plan.orders[part][0]:
                    pairs.append((x, got_e))
                else:
                    outs = (plan.tile(2 * nb << step),)
                    (x,) = call(join_body, (x, got_e), outs, placed=False)
        tail = ((rows // 2 + (8 if op else 0), cols), F32)
        acc = ()
        for far in (0, 1):
            ins = [x for pair in kept for x in pair] + [scale] + [pair[far] for pair in pairs]
            outs = [tail, tail] if far else [square]
            if op:
                ins += [pair[far] for pair in earlier] + [more]
                outs.append(lines)
            if far:
                ins += [*acc, term, keep_p, gather_hot]
            acc = call(
                lambda *r, far=far: values_body(plan, far, *r),
                (place, *ins),
                outs,
                scratch=full,
                flops=work // 2,
            )
        own, other, *sums = acc
        value = own + swap(other, "snp", 1)
        for bit in bits_of(blocks)[1:]:
            value = value + swap(value, "snp", bit)
        after = (more, sums[0]) if op else (more, pairs)
        return value, swap(value, "snp", 1), *after

    own, other, plain, earlier = round_trip(0, plan, right_side, messages, (), None)
    image, flipped, sums, *messages = call(
        lambda *r: middle_body(summing, *r),
        (place, right_side, diagonal, own, other, *kept[0], gather_turned),
        (square, *turned, *summing.message_shapes(groups[0])),
        scratch=full,
        flops=work,
    )
    for index, group in enumerate(groups[1:]):
        messages += call(
            lambda *r, group=group: more_body(plan, group, *r),
            (*kept[index + 1], flipped, sums),
            plan.message_shapes(group),
            flops=work,
            placed=False,
        )
    own, other, dots, more = round_trip(
        1, summing, image, messages, (plain, diagonal, right_side), earlier
    )
    return call(
        final_body,
        (place, image, diagonal, own, other, right_side, dots, more),
        (square, square),
        scratch=full,
    )


def solution(mesh):
    placed = (
        P("animal", "snp"),
        P("snp"),
        P("animal", None),
        P("animal", None),
        P("animal"),
        P(),
        P("animal", None, None),
        P("animal"),
        P("animal"),
    )

    return jax.shard_map(
        local,
        mesh=mesh,
        in_specs=placed,
        out_specs=(P("animal", None), P("animal", None)),
        check_vma=False,
    )
```

```python
import jax
import jax.numpy as jnp
from jax import lax
from jax.experimental import pallas as pl
from jax.experimental.pallas import tpu as pltpu
from jax.sharding import PartitionSpec as P


BF16, F32, I32 = jnp.bfloat16, jnp.float32, jnp.int32
LANES = 128
VMEM = pl.BlockSpec(memory_space=pltpu.VMEM)
SMEM = pl.BlockSpec(memory_space=pltpu.SMEM)
HBM = pl.BlockSpec(memory_space=pltpu.HBM)


def call(body, ins, outs, specs=None, limit=24, scratch=(), flops=0,
         placed=True):
    specs = specs or [VMEM] * (len(ins) - 1)
    outs = tuple(o if hasattr(o, "memory_space") else jax.ShapeDtypeStruct(*o) for o in outs)
    moved = sum(a.size * a.dtype.itemsize for a in ins)
    return pl.pallas_call(
        body,
        in_specs=[SMEM, *specs] if placed else [VMEM] * len(ins),
        out_specs=tuple(VMEM for _ in outs),
        out_shape=outs,
        scratch_shapes=scratch,
        cost_estimate=pl.CostEstimate(flops=flops, bytes_accessed=moved, transcendentals=0),
        compiler_params=pltpu.CompilerParams(vmem_limit_bytes=limit << 20),
    )(*ins)


def positions(order):
    if not order:
        return [0]
    rest = positions(order[1:])
    return rest + [j | order[0] for j in rest]


def swap(x, axis, bit):
    size = lax.axis_size(axis)
    return lax.ppermute(x, axis, [(i, i ^ bit) for i in range(size)])


def bits_of(size):
    return [1 << b for b in range(size.bit_length() - 1)]


def part_count(owned):
    return max(1, min(4, owned // LANES))


def colsum(x):
    return jnp.sum(x, axis=0, keepdims=True)


def stack_rows(rows):
    wide = rows[0].shape[1]
    return jnp.concatenate([*rows, jnp.zeros((8 - len(rows), wide), F32)], axis=0)


def split(x):
    high = x.astype(BF16)
    return high, (x - high.astype(F32)).astype(BF16)


def hot_dot(hot, x, dims):
    high, low = split(x)
    dims = (dims, ((), ()))
    out = lax.dot_general(hot, high, dims, preferred_element_type=F32)
    return out + lax.dot_general(hot, low, dims, preferred_element_type=F32)


class Plan:
    def __init__(self, genotype, right_side, send_rows, carry):
        self.owners = lax.axis_size("animal")
        self.rows, self.snps = genotype.shape
        self.cols = right_side.shape[1]
        self.slots = send_rows.shape[2]
        self.half = self.owners // 2
        self.owned = self.snps // self.owners
        self.parts = part_count(self.owned)
        self.width = self.owned // self.parts
        self.nb = self.width // LANES
        bits = bits_of(self.owners)
        flip = [bits[1], bits[0], *bits[2:]]
        early = [bits[0], *bits[2:], bits[1]]
        self.orders = [bits, flip, early, flip][: self.parts]
        self.bits = bits
        self.sets = [[0, 1], [2, 3]] if self.parts == 4 else [list(range(self.parts))]

        self.groups = lax.axis_size("snp")
        self.kinds = max(1, self.groups // 2)
        self.lane_shift = (self.cols // self.groups).bit_length() - 1
        self.packed = self.slots // self.kinds
        self.pedigree = self.owners * self.packed
        self.carry = carry
        self.line = self.packed + carry

    def tile(self, blocks, slots=0):
        return ((blocks * LANES + slots * self.line, self.cols), BF16)

    def message_shapes(self, group):
        half, nb = self.half, self.nb
        shapes = []
        for part in group:
            if part:
                shapes += [self.tile(half * nb), self.tile(half * nb)]
            else:
                shapes += [self.tile(half * nb, half), self.tile(half * nb), self.tile(0, half)]
        return shapes

    def share(self, group):
        return self.width * len(group)

    def kept_shapes(self, group):
        wide = self.owners * self.share(group)
        return [pltpu.VMEM((self.rows, wide), BF16), ((1, wide), F32)]

    def lane_group(self, shape):
        return lax.broadcasted_iota(I32, shape, 1) >> self.lane_shift

    def fold(self, x):
        shift = self.cols // 2
        while shift >> self.lane_shift:
            x = x + pltpu.roll(x, shift, 1)
            shift //= 2
        return x

    def mine(self, place, x):
        return jnp.where(self.lane_group(x.shape) == place[1], x, 0.0)

    def mix(self, x):
        high = x.astype(BF16).astype(F32)
        return jnp.where(self.lane_group(x.shape) < self.kinds, high, x - high)

    def select(self, pieces):
        kind = self.lane_group(pieces[0].shape) & (self.kinds - 1)
        out = pieces[0]
        for k in range(1, self.kinds):
            out = jnp.where(kind == k, pieces[k], out)
        return out

    def pack(self, x):
        size = self.pedigree
        pieces = [x[k * size : (k + 1) * size] for k in range(self.kinds)]
        return self.select(pieces).astype(BF16)


def encode(plan, rows):
    lines = []
    for row in rows:
        high = row.astype(BF16).astype(F32)
        mid = (row - high).astype(BF16).astype(F32)
        lines += [high, mid, row - high - mid]
    lines.append(jnp.zeros((plan.carry - len(lines), plan.cols), F32))
    return jnp.concatenate(lines, axis=0).astype(BF16)


def decode(total, count):
    return [colsum(total[3 * i : 3 * i + 3]) for i in range(count)]


def put_rows(plan, order, packed, send, offset, keep, sums=None):
    size = plan.packed
    for at, r in enumerate(positions(order)):
        block = packed[r * size : (r + 1) * size]
        out, first = keep, at * plan.line
        if at >= plan.half:
            out, first = send, offset + (at - plan.half) * plan.line
        out[first : first + size] = block
        if sums is not None:
            out[first + size : first + plan.line] = sums


def take_rows(plan, keep_p, got, edge):
    blocks, sums = [], None
    for at in range(plan.owners):
        from_, first = keep_p, at * plan.line
        if at >= plan.half:
            from_, first = got, edge + (at - plan.half) * plan.line
        blocks.append(from_[first : first + plan.packed])
        if plan.carry:
            under = from_[first + plan.packed : first + plan.line].astype(F32)
            sums = under if sums is None else sums + under
    return blocks, sums


def copy_in(plan, group, place, geno, freq, kept, kept_freq, sem, freq_sem):
    wide = plan.share(group)
    copies = []
    for r in range(plan.owners):
        first = (place[0] ^ r) * plan.owned + group[0] * plan.width
        there = pl.ds(pl.multiple_of(first, LANES), wide)
        here = pl.ds(r * wide, wide)
        copies.append((
            pltpu.make_async_copy(freq.at[:, there], kept_freq.at[:, here], freq_sem.at[r]),
            pltpu.make_async_copy(geno.at[:, there], kept.at[:, here], sem.at[r]),
        ))
        for copy in copies[-1]:
            copy.start()
    return copies


def put_effects(plan, group, r, geno, freq, turned, sums, messages):
    wide = plan.share(group)
    here = slice(r * wide, (r + 1) * wide)
    acc = jnp.dot(turned, geno[:, here], preferred_element_type=F32)
    acc = (acc - sums * (2.0 * freq[:, here])).astype(BF16)
    half, nb = plan.half, plan.nb
    messages = list(messages)
    for index, part in enumerate(group):
        send, keep = messages[:2]
        messages = messages[2 if part else 3 :]
        at = positions(plan.orders[part]).index(r)
        out, at = (keep, at) if at < half else (send, at - half)
        for b in range(nb):
            first = index * plan.width + b * LANES
            row = (at * nb + b) * LANES
            out[row : row + LANES] = acc[:, first : first + LANES]


def emit_rows(plan, place, field, gather_turned, messages, sums=None):
    mixed = plan.mix(plan.fold(plan.mine(place, field))).astype(BF16)
    rows = jnp.dot(gather_turned[...], mixed, preferred_element_type=F32)
    offset = plan.half * plan.nb * LANES
    put_rows(plan, plan.bits, plan.pack(rows), messages[0], offset, messages[2], sums)


def turn(field):
    turned = field.T.astype(BF16)
    return turned, jnp.sum(turned.astype(F32), axis=1, keepdims=True)


def fill_index(plan, place, send_rows, index):
    packed = plan.packed
    for r in range(plan.owners):
        line = send_rows[pl.ds(place[0] ^ r, 1), :]
        for k in range(plan.kinds):
            first = k * plan.pedigree + r * packed
            index[:, first : first + packed] = line[:, k * packed : (k + 1) * packed]


def turn_out(field, flipped, sums):
    turned, side = turn(field)
    flipped[...] = turned
    sums[...] = jnp.broadcast_to(side, sums.shape)
    return turned, side


def begin_body(plan, place, geno, freq, right_in, send_in,
               kept, kept_freq, gather_turned, flipped, sums, *rest):
    messages, scratch = rest[:-6], rest[-6:]
    right, send_rows, index, sem, freq_sem, small_sem = scratch
    pairs = ((send_in, send_rows), (right_in, right))
    small = [pltpu.make_async_copy(*pair, small_sem.at[i]) for i, pair in enumerate(pairs)]
    for copy in small:
        copy.start()
    group = plan.sets[0]
    copies = copy_in(plan, group, place, geno, freq, kept, kept_freq, sem, freq_sem)
    small[0].wait()
    fill_index(plan, place, send_rows, index)
    tall = jnp.broadcast_to(index[...].astype(F32), (LANES, index.shape[1])).T
    lane = lax.broadcasted_iota(I32, tall.shape, 1).astype(F32)
    for first in range(0, plan.rows, LANES):
        hot = jnp.where(lane + first == tall, 1.0, 0.0)
        gather_turned[:, first : first + LANES] = hot.astype(BF16)
    small[1].wait()
    emit_rows(plan, place, right[...], gather_turned, messages)
    turned, side = turn_out(right[...], flipped, sums)
    for r in range(plan.owners):
        for copy in copies[r]:
            copy.wait()
        put_effects(plan, group, r, kept, kept_freq, turned, side, messages)


def tables_body(plan, place, sire, dam, mendelian, send_rows, parent_hot, parent_turned, weight,
                gather_hot, index):
    me, slots, packed = place[0], plan.slots, plan.packed
    shift, short = slots.bit_length() - 1, packed.bit_length() - 1

    def spot(slot):
        owner, row = (slot >> shift) ^ me, slot & (slots - 1)
        return (row >> short) * plan.pedigree + (owner << short) + (row & (packed - 1))

    def column(line):
        return jnp.broadcast_to(line, (LANES, plan.rows)).T

    sires, dams = spot(sire[...]), spot(dam[...])
    tall = [column(x.astype(F32)) for x in (sires, dams)]
    weight[...] = column(mendelian[...])
    fill_index(plan, place, send_rows, index)
    animal = lax.broadcasted_iota(I32, (plan.rows, LANES), 0)
    row = lax.broadcasted_iota(I32, (LANES, plan.rows), 0)
    lane = lax.broadcasted_iota(I32, (plan.rows, LANES), 1).astype(F32)
    for first in range(0, plan.owners * slots, LANES):
        here = slice(first, first + LANES)
        hot = jnp.where(row == sires - first, 1.0, 0.0) + jnp.where(row == dams - first, 1.0, 0.0)
        parent_hot[here, :] = hot.astype(BF16)
        hot = jnp.where(lane + first == tall[0], 1.0, 0.0)
        hot = hot + jnp.where(lane + first == tall[1], 1.0, 0.0)
        parent_turned[:, here] = hot.astype(BF16)
        gather_hot[:, here] = jnp.where(animal == index[:, here], 1.0, 0.0).astype(BF16)


def begin_more_body(plan, group, place, geno, freq, flipped, sums, kept, kept_freq, *rest):
    messages, (sem, freq_sem) = rest[:-2], rest[-2:]
    copies = copy_in(plan, group, place, geno, freq, kept, kept_freq, sem, freq_sem)
    for r in range(plan.owners):
        for copy in copies[r]:
            copy.wait()
        put_effects(plan, group, r, kept, kept_freq, flipped[...], sums[:, :1], messages)


def more_body(plan, group, geno, freq, flipped, sums, *messages):
    for r in range(plan.owners):
        put_effects(plan, group, r, geno, freq, flipped[...], sums[:, :1], messages)


def merge_body(plan, slots_left, sources, got, keep_e, keep_p, send, next_e, next_p):
    half = slots_left // 2
    count = slots_left * plan.nb * LANES
    summed = (keep_e[...].astype(F32) + got[0:count].astype(F32)).astype(BF16)
    next_e[...] = summed[: count // 2]
    send[0 : count // 2] = summed[count // 2 :]
    size, step = half * plan.line, slots_left * plan.line
    for s in range(2 * sources):
        from_, at = (keep_p, s * step) if s < sources else (got, count + (s - sources) * step)
        next_p[s * size : (s + 1) * size] = from_[at : at + size]
        first = count // 2 + s * size
        send[first : first + size] = from_[at + size : at + step]


def add_body(got, keep, *out):
    summed = (keep[...].astype(F32) + got[...].astype(F32)).astype(BF16)
    size = summed.shape[0] // len(out)
    for i, ref in enumerate(out):
        ref[...] = summed[i * size : (i + 1) * size]


def join_body(sent, got, out):
    size = sent.shape[0]
    out[0:size] = sent[...]
    out[size:] = got[...]


def offspring_body(plan, second, place, got, keep_e, keep_p, field, parent_hot, parent_turned,
                   weight, *rest):
    if second:
        plain_before, diagonal, right, *rest = rest
    send, keep_back, term, extra = rest
    edge, size = plan.nb * LANES, plan.pedigree
    send[0:edge] = (keep_e[...].astype(F32) + got[0:edge].astype(F32)).astype(BF16)
    blocks, under = take_rows(plan, keep_p, got, edge)
    received = jnp.concatenate(blocks, axis=0)
    pieces = [
        jnp.dot(parent_turned[:, k * size : (k + 1) * size], received, preferred_element_type=F32)
        for k in range(plan.kinds)
    ]
    parents = plan.fold(plan.select(pieces))
    plain = plan.fold(plan.mine(place, field[...])) - 0.5 * parents
    mendel = weight[...] * plain
    term[...] = mendel
    back = -0.5 * hot_dot(parent_hot[...], mendel, ((1,), (0,)))
    sums = None
    if second:
        gamma, delta = decode(under, 2)
        extra[...] = stack_rows([gamma, delta])
        alpha = gamma / delta
        residual = right[...] - alpha * field[...]
        moved = plain_before[...] - alpha * plain
        sums = encode(plan, [
            colsum(residual * residual),
            colsum(field[...] * residual),
            colsum(diagonal[...] * field[...] * residual),
            plan.mine(place, colsum(mendel * moved)),
        ])
    else:
        extra[...] = plain
    put_rows(plan, plan.bits[::-1], plan.pack(plan.mix(back)), send, edge, keep_back, sums)


def spread_body(plan, slots_held, sources, sent, got, keep_p, send, next_p):
    count = slots_held * plan.nb * LANES
    send[0:count] = sent[0:count]
    send[count : 2 * count] = got[0:count]
    step = plan.half // sources * plan.line
    size = step // 2
    for s in range(2 * sources):
        from_, at = (keep_p, s * step) if s < sources else (got, count + (s - sources) * step)
        next_p[s * size : (s + 1) * size] = from_[at : at + size]
        first = 2 * count + s * size
        send[first : first + size] = from_[at + size : at + step]


def home_rows(plan, place, term, keep_p, got, gather_hot):
    blocks, under = take_rows(plan, keep_p, got, plan.half * plan.nb * LANES)
    order = positions(plan.bits)
    returned = jnp.concatenate([blocks[order.index(r)] for r in range(plan.owners)], axis=0)
    size = plan.pedigree
    pieces = [
        jnp.dot(gather_hot[:, k * size : (k + 1) * size], returned, preferred_element_type=F32)
        for k in range(plan.kinds)
    ]
    return plan.mine(place, term[...] + plan.fold(plan.select(pieces))), under


def lane_total(plan, x):
    side = jnp.sum(x, axis=1, keepdims=True)
    return jnp.broadcast_to(side, (plan.cols, LANES)).T[0:1, :]


def stage_sets(plan, stage):
    return plan.sets if stage == 0 else [plan.sets[stage - 1]]


def values_body(plan, stage, place, *refs):
    second, far, final = plan.carry > 0, stage > 0, stage == len(plan.sets)
    sets = stage_sets(plan, stage)
    parts = [part for group in sets for part in group]
    kept, refs = refs[: 2 * len(sets)], refs[2 * len(sets) :]
    scale, refs = refs[0], refs[1:]
    held, refs = dict(zip(parts, refs)), refs[len(parts) :]
    if second:
        earlier, dots, refs = dict(zip(parts, refs)), refs[len(parts)], refs[len(parts) + 1 :]
        alpha = dots[0:1, :] / dots[1:2, :]
        alpha = jnp.broadcast_to(alpha, (LANES, plan.cols)).T[:, :1]
    if far:
        before, refs = refs[0], refs[1:]
        if second:
            lines_before, refs = refs[0], refs[1:]
    if stage == 1:
        term, keep_p, gather_hot, *refs = refs
    *outs, acc = refs
    turned = (((1,), (1,)), ((), ()))
    nb, half = plan.nb, plan.half

    def block_of(ref, at):
        tiles = [ref[(at * nb + b) * LANES : (at * nb + b + 1) * LANES] for b in range(nb)]
        return jnp.concatenate(tiles, axis=1)

    spread, inner = None, None
    for number, group in enumerate(sets):
        geno, freq = kept[2 * number : 2 * number + 2]
        for index, part in enumerate(group):
            order = positions(plan.orders[part])
            for at, r in enumerate(order[half:] if far else order[:half]):
                first_column = r * plan.share(group) + index * plan.width
                here = slice(first_column, first_column + plan.width)
                block = block_of(held[part], at)
                wide = block.astype(F32)
                off = wide * (2.0 * freq[:, here])
                if second:
                    product = wide * (block_of(earlier[part], at).astype(F32) - alpha * wide)
                    inner = product if inner is None else inner + product
                value = lax.dot_general(
                    geno[:, here], block, turned, preferred_element_type=F32
                )
                if spread is None:
                    spread, acc[...] = off, value
                else:
                    spread = spread + off
                    acc[...] += value
    values = scale[...] * (acc[...] - lane_total(plan, spread))
    if second:
        inner = scale[...] * lane_total(plan, inner)
    if far:
        values = before[...] + values
    carried = []
    if stage == 1:
        home, under = home_rows(plan, place, term, keep_p, held[0], gather_hot)
        values = values + home
        if second:
            gamma, cross, own_part, pedigree = decode(under, 4)
            inner = inner + lines_before[0:1, :] + pedigree
            carried = [gamma, cross, own_part]
    elif far and second:
        inner = inner + lines_before[0:1, :]
        carried = [lines_before[i : i + 1, :] for i in (1, 2, 3)]
    if second:
        outs[-1][...] = stack_rows([inner, *carried])
    if not final:
        outs[0][...] = values
        return
    acc[...] = values
    own, other = outs[:2]
    rows = plan.rows // 2
    at = (place[1] & 1) * rows
    own[0:rows] = acc[pl.ds(pl.multiple_of(at, rows), rows), :]
    other[0:rows] = acc[pl.ds(pl.multiple_of(rows - at, rows), rows), :]
    if second:
        own[rows:] = stack_rows([inner])
        other[rows:] = stack_rows([inner])


def apply_operator(place, field, diagonal, own, other, full):
    rows = field.shape[0] // 2
    at = (place[1] & 1) * rows
    full[pl.ds(pl.multiple_of(at, rows), rows), :] = own[0:rows]
    full[pl.ds(pl.multiple_of(rows - at, rows), rows), :] = other[0:rows]
    return diagonal[...] * field[...] + full[...]


def middle_body(plan, place, field, diagonal, own, other, geno, freq, gather_turned,
                image, flipped, sums, *rest):
    messages, full = rest[:-1], rest[-1]
    out = apply_operator(place, field, diagonal, own, other, full)
    image[...] = out
    dots = encode(plan, [colsum(field[...] * field[...]), colsum(out * field[...])])
    emit_rows(plan, place, image[...], gather_turned, messages, dots)
    turned, side = turn_out(image[...], flipped, sums)
    for r in range(plan.owners):
        put_effects(plan, plan.sets[0], r, geno, freq, turned, side, messages)


def final_body(place, field, diagonal, own, other, right, dots, more,
               solution, residual, full):
    q = apply_operator(place, field, diagonal, own, other, full)
    alpha0 = dots[0:1, :] / dots[1:2, :]
    gamma = more[1:2, :]
    rows = field.shape[0] // 2
    delta = more[2:3, :] - alpha0 * (more[3:4, :] + own[rows : rows + 1, :])
    beta = gamma / dots[0:1, :]
    alpha = gamma / (delta - beta * gamma / alpha0)
    left = right[...] - alpha0 * field[...]
    w = field[...] - alpha0 * q
    s = w + beta * field[...]
    p = left + beta * right[...]
    solution[...] = alpha0 * right[...] + alpha * p
    residual[...] = left - alpha * s


def local(genotype, allele_freq, right_side, diagonal, mendelian, genomic_weight, send_rows,
          sire_slot, dam_slot):
    blocks = lax.axis_size("snp")
    plan = Plan(genotype, right_side, send_rows, 0)
    summing = Plan(genotype, right_side, send_rows, 16)
    rows, cols, half, nb, parts = plan.rows, plan.cols, plan.half, plan.nb, plan.parts
    place = jnp.stack([lax.axis_index("animal"), lax.axis_index("snp")]).astype(I32)
    freq = allele_freq.reshape(1, plan.snps)
    scale = (genomic_weight / (plan.snps * blocks)).reshape(1, cols)
    square = ((rows, cols), F32)
    lines = ((8, cols), F32)
    wide = plan.owners * plan.slots
    work = 2 * rows * cols * plan.snps
    groups = plan.sets
    turned = (((cols, rows), BF16), ((cols, LANES), F32))
    full = [pltpu.VMEM((rows, cols), F32)]

    whole, frequency = (
        pltpu.with_memory_space_constraint(x, pltpu.HBM) for x in (genotype, freq)
    )
    copies = [pltpu.SemaphoreType.DMA((plan.owners,))] * 2
    geno, freq, gather_turned, flipped, sums, *messages = call(
        lambda *r: begin_body(plan, *r),
        (place, whole, frequency, *[
            pltpu.with_memory_space_constraint(x, pltpu.HBM)
            for x in (right_side, send_rows[0])
        ]),
        (*plan.kept_shapes(groups[0]), ((wide, rows), BF16), *turned,
         *plan.message_shapes(groups[0])),
        specs=[HBM] * 4,
        scratch=[
            pltpu.VMEM((rows, cols), F32),
            pltpu.VMEM(send_rows.shape[1:], I32),
            pltpu.VMEM((1, wide), I32),
            *copies,
            pltpu.SemaphoreType.DMA((2,)),
        ],
        flops=work,
    )
    *tables, gather_hot = call(
        lambda *r: tables_body(plan, *r),
        (place, sire_slot.reshape(1, rows), dam_slot.reshape(1, rows), mendelian.reshape(1, rows),
         send_rows[0]),
        (((wide, rows), BF16), ((rows, wide), BF16), square, ((rows, wide), BF16)),
        scratch=[pltpu.VMEM((1, wide), I32)],
    )
    kept = [(geno, freq)]
    for group in groups[1:]:
        *pair, = call(
            lambda *r, group=group: begin_more_body(plan, group, *r),
            (place, whole, frequency, flipped, sums),
            (*plan.kept_shapes(group), *plan.message_shapes(group)),
            specs=[HBM] * 2 + [VMEM] * 2,
            scratch=copies,
            flops=work,
        )
        kept.append(tuple(pair[:2]))
        messages += pair[2:]

    def round_trip(op, plan, field, messages, extra, earlier):
        order = plan.bits
        send, keep_e, keep_p = messages[:3]
        left, sources = half, 1
        got = swap(send, "animal", order[0])
        for bit in order[1:]:
            send, keep_e, keep_p = call(
                lambda *r, left=left, sources=sources: merge_body(plan, left, sources, *r),
                (got, keep_e, keep_p),
                (plan.tile(left // 2 * nb, half), plan.tile(left // 2 * nb), plan.tile(0, half)),
                placed=False,
            )
            left, sources = left // 2, sources * 2
            got = swap(send, "animal", bit)
        others = []
        for part in range(1, parts):
            other, keep = messages[2 * part + 1 : 2 * part + 3]
            for i, bit in enumerate(plan.orders[part]):
                got_e = swap(other, "animal", bit)
                size = half >> i
                outs = (plan.tile(size // 2 * nb),) * 2 if size > 1 else (plan.tile(nb),)
                keep, *other = call(add_body, (got_e, keep), outs, placed=False)
                other = other[0] if other else None
            others.append(keep)
        sent, keep_p, term, more = call(
            lambda *r: offspring_body(plan, bool(extra), *r),
            (place, got, keep_e, keep_p, field, *tables, *extra),
            (plan.tile(nb, half), plan.tile(0, half), square, lines if extra else square),
        )
        got = swap(sent, "animal", order[-1])
        held, sources = 1, 1
        for bit in order[-2::-1]:
            sent, keep_p = call(
                lambda *r, held=held, sources=sources: spread_body(plan, held, sources, *r),
                (sent, got, keep_p),
                (plan.tile(2 * held * nb, half), plan.tile(0, half)),
                placed=False,
            )
            held, sources = held * 2, sources * 2
            got = swap(sent, "animal", bit)
        pairs = [(sent, got)]
        for part in range(1, parts):
            x = others[part - 1]
            for step, bit in enumerate(plan.orders[part][::-1]):
                got_e = swap(x, "animal", bit)
                if bit == plan.orders[part][0]:
                    pairs.append((x, got_e))
                else:
                    outs = (plan.tile(2 * nb << step),)
                    (x,) = call(join_body, (x, got_e), outs, placed=False)
        tail = ((rows // 2 + (8 if op else 0), cols), F32)
        acc = ()
        for stage in range(len(groups) + 1):
            used = [part for group in stage_sets(plan, stage) for part in group]
            stores = kept if stage == 0 else [kept[stage - 1]]
            far = min(stage, 1)
            ins = [x for pair in stores for x in pair] + [scale]
            ins += [pairs[part][far] for part in used]
            outs = [tail, tail] if stage == len(groups) else [square]
            if op:
                ins += [earlier[part][far] for part in used] + [more]
                outs.append(lines)
            ins += acc
            if stage == 1:
                ins += [term, keep_p, gather_hot]
            acc = call(
                lambda *r, stage=stage: values_body(plan, stage, *r),
                (place, *ins),
                outs,
                scratch=full,
                flops=work * len(used) // (2 * parts),
            )
        own, other, *sums = acc
        value = own + swap(other, "snp", 1)
        for bit in bits_of(blocks)[1:]:
            value = value + swap(value, "snp", bit)
        after = (more, sums[0]) if op else (more, pairs)
        return value, swap(value, "snp", 1), *after

    own, other, plain, earlier = round_trip(0, plan, right_side, messages, (), None)
    image, flipped, sums, *messages = call(
        lambda *r: middle_body(summing, *r),
        (place, right_side, diagonal, own, other, *kept[0], gather_turned),
        (square, *turned, *summing.message_shapes(groups[0])),
        scratch=full,
        flops=work,
    )
    for index, group in enumerate(groups[1:]):
        messages += call(
            lambda *r, group=group: more_body(plan, group, *r),
            (*kept[index + 1], flipped, sums),
            plan.message_shapes(group),
            flops=work,
            placed=False,
        )
    own, other, dots, more = round_trip(
        1, summing, image, messages, (plain, diagonal, right_side), earlier
    )
    return call(
        final_body,
        (place, image, diagonal, own, other, right_side, dots, more),
        (square, square),
        scratch=full,
    )


def solution(mesh):
    placed = (
        P("animal", "snp"),
        P("snp"),
        P("animal", None),
        P("animal", None),
        P("animal"),
        P(),
        P("animal", None, None),
        P("animal"),
        P("animal"),
    )

    return jax.shard_map(
        local,
        mesh=mesh,
        in_specs=placed,
        out_specs=(P("animal", None), P("animal", None)),
        check_vma=False,
    )
```
